512 devices in a mesh: lon: 32 (over z, x_lo, core), lat: 16 (over x_hi, y).
Axes of the slice: x: 4 (x_hi: 2, x_lo: 2; x = x_hi * 2 + x_lo), y: 8, z: 8, core: 2. Of those that a mesh axis runs over, the one named last changes fastest.
Arguments:
- queries: float32 [128, 512, 1024], P('lat', 'lon'), may hold values from -400 to 400
- key_vectors: float32 [128, 512, 1024], P('lat', 'lon'), may hold values from -10 to 10
- value_vectors: float32 [128, 512, 1024], P('lat', 'lon'), may hold values from -6 to 6
- land_mask: int32 [128, 512], P('lat', 'lon'), may hold values from 0 to 1, as said below
- radius: int32 [16], replicated, may hold values from 1 to 4, as said below
- offsets: int32 [2, 2, 16], replicated, may hold values from 0 to 3
Outputs:
- attended: float32 [128, 512, 1024], P('lat', 'lon')
The draws below stay inside these ranges and needn't reach their ends.
Inputs may be any that keep to these rules, and one draw needn't show every extreme that they name: `land_mask`: 1 marks land, 0 water. Some head has radius 4 and some head radius 1.
All inputs are finite; a program needn't handle non-finite values.
Results may differ from the reference program's by a relative error of at most 0.0003.
Values sent between devices are 32-bit elements; how exact they have to be, the bound alone decides.
No kernel may reach another device: no remote copies, remote signals or barrier semaphores. Data moves between devices by JAX's collectives and lax.ppermute only.
A program may use at most 64 MiB of HBM per device.

```python
import math
import jax
import jax.numpy as jnp
from jax import lax

D = 1024
HEADS = 16
TH = 8
TW = 16
HALO = 4
RATE = 4
LEVELS = 2
NLAT = 128
NLON = 512
N_LON = 32
N_LAT = 16


def land_pattern(key):
    raw_bits = jax.random.randint(jax.random.fold_in(key, 701), (NLAT, NLON), 0, 10)
    return (raw_bits < 7).astype(jnp.int32)


def drawn_keys(key):
    return jax.random.normal(jax.random.fold_in(key, 702), (NLAT, NLON, D), jnp.float32)


def draw_land_mask(key, part):
    return land_pattern(key)


def draw_key_vectors(key, part):
    normal_draw = drawn_keys(key)
    return normal_draw


def draw_queries(key, part):
    normal_draw = jax.random.normal(jax.random.fold_in(key, 703), (NLAT, NLON, D), jnp.float32)
    return normal_draw


def draw_radius(key, part):
    raw_radius = jax.random.randint(jax.random.fold_in(key, 704), (HEADS,), 1, HALO + 1)
    ordering = jax.random.permutation(jax.random.fold_in(key, 705), HEADS)
    return raw_radius.at[ordering[0]].set(HALO).at[ordering[1]].set(1).astype(jnp.int32)


def plant(result, own_key, least, top_value):
    extent = result.shape
    index_at = [jax.random.randint(jax.random.fold_in(own_key, axis), (), 0, extent[axis]) for axis in range(len(extent))]
    result = result.at[tuple(index_at)].set(least)
    longest = extent.index(max(extent))
    index_at[longest] = (index_at[longest] + 1) % extent[longest]
    return result.at[tuple(index_at)].set(top_value)


def block_levels(own_key, extent, cuts, low, largest):
    def one(dim, parts):
        draws = jax.random.uniform(jax.random.fold_in(jax.random.fold_in(own_key, 6), dim), (parts,), jnp.float32, low / len(cuts), largest / len(cuts))
        return jnp.repeat(jnp.exp(draws), extent[dim] // parts).reshape((-1,) + (1,) * (len(extent) - dim - 1))

    factor_of = one(*cuts[0])
    for cut in cuts[1:]:
        factor_of = factor_of * one(*cut)
    return factor_of


def gaussian(key, dims, deviation, limit, pieces=(), kind=jnp.bfloat16):
    gain = block_levels(key, dims, pieces, -0.22, 0.18) if pieces else 1.0
    entries = jax.random.normal(key, dims, jnp.float32) * deviation * gain
    return jnp.minimum(jnp.maximum(entries, -limit), limit).astype(kind)


def setup_inputs(seed: int = 0) -> dict:
    streams_of = jax.random.split(jax.random.key(seed), 7)
    return {
        "queries": draw_queries(jax.random.fold_in(streams_of[6], 71), 0),
        "key_vectors": draw_key_vectors(jax.random.fold_in(streams_of[6], 71), 0),
        "value_vectors": gaussian(streams_of[2], (NLAT, NLON, D), 1.0, 6.0, ((0, 16), (1, 32)), jnp.float32),
        "land_mask": draw_land_mask(jax.random.fold_in(streams_of[6], 71), 0),
        "radius": draw_radius(jax.random.fold_in(streams_of[6], 71), 0),
        "offsets": plant(jax.random.randint(streams_of[5], (LEVELS, 2, HEADS), 0, RATE), jax.random.fold_in(streams_of[5], 1), 0, RATE - 1).astype(jnp.int32),
    }


def pick_rows(key_flat, value_flat, land_flat, chosen):
    token_count, features = key_flat.shape
    head_count = chosen.shape[0]
    head_size = features // head_count
    segment_rows = token_count // RATE
    index_grid = jnp.broadcast_to(chosen.reshape(1, 1, head_count, 1), (segment_rows, 1, head_count, 1))

    def select(source):
        shaped = source.reshape(segment_rows, RATE, head_count, head_size)
        return jnp.take_along_axis(shaped, index_grid, axis=1).reshape(segment_rows, features)
    land_grid = land_flat.reshape(segment_rows, RATE)
    land_index = jnp.broadcast_to(chosen.reshape(1, head_count), (segment_rows, head_count))
    return (select(key_flat), select(value_flat), jnp.take_along_axis(land_grid, land_index, axis=1))

def attend(queries, near_keys, near_values, near_land, far_keys, far_values, far_land, radius, tile_cols):
    token_count, features = queries.shape
    head_count = radius.shape[0]
    head_size = features // head_count
    group_size = math.gcd(head_count, 8)
    group_count = head_count // group_size
    group_width = group_size * head_size
    extended_cols = tile_cols + 2 * HALO
    query_spot = jnp.arange(token_count, dtype=jnp.int32)
    query_row = query_spot // tile_cols + HALO
    query_col = query_spot % tile_cols + HALO
    key_spot = jnp.arange(near_keys.shape[0], dtype=jnp.int32)
    key_row = key_spot // extended_cols
    key_col = key_spot % extended_cols
    spacing = jnp.maximum(jnp.abs(query_row[:, None] - key_row[None, :]), jnp.abs(query_col[:, None] - key_col[None, :]))
    land_okay = (near_land[None, :] == 1) | (spacing == 0)
    scale_by = 1.0 / math.sqrt(head_size)
    highest = lax.Precision.HIGHEST

    def group_slice(source, group_at):
        piece = lax.dynamic_slice_in_dim(source, (group_at * group_width).astype(jnp.int32), group_width, 1)
        return piece.reshape(source.shape[0], group_size, head_size)

    def one_group(group_at):
        query_group = group_slice(queries, group_at)
        near_key_group = group_slice(near_keys, group_at)
        near_value_group = group_slice(near_values, group_at)
        far_key_group = group_slice(far_keys, group_at)
        far_value_group = group_slice(far_values, group_at)
        group_radius = lax.dynamic_slice_in_dim(radius, (group_at * group_size).astype(jnp.int32), group_size, 0)
        near_score = jnp.einsum('tgd,kgd->gtk', query_group, near_key_group, precision=highest, preferred_element_type=jnp.float32) * scale_by
        allowed = land_okay[None, :, :] & (spacing[None, :, :] <= group_radius[:, None, None])
        near_score = jnp.where(allowed, near_score, -jnp.inf)
        far_score = jnp.einsum('tgd,kgd->gtk', query_group, far_key_group, precision=highest, preferred_element_type=jnp.float32) * scale_by
        far_okay = lax.dynamic_slice_in_dim(far_land, (group_at * group_size).astype(jnp.int32), group_size, 1).T == 1
        far_score = jnp.where(far_okay[:, None, :], far_score, -jnp.inf)
        top_score = jnp.maximum(lax.optimization_barrier(jnp.max(near_score, axis=2)), lax.optimization_barrier(jnp.max(far_score, axis=2)))
        near_weight = jnp.exp(near_score - top_score[:, :, None])
        far_weight = jnp.exp(far_score - top_score[:, :, None])
        total = lax.optimization_barrier(jnp.sum(near_weight, axis=2)) + lax.optimization_barrier(jnp.sum(far_weight, axis=2))
        mixed = jnp.einsum('gtk,kgd->tgd', near_weight, near_value_group, precision=highest, preferred_element_type=jnp.float32)
        mixed = mixed + jnp.einsum('gtk,kgd->tgd', far_weight, far_value_group, precision=highest, preferred_element_type=jnp.float32)
        mixed = mixed / total.T[:, :, None]
        return mixed.reshape(token_count, group_width)
    per_group = lax.map(one_group, jnp.arange(group_count, dtype=jnp.int32))
    return per_group.transpose(1, 0, 2).reshape(token_count, features)

def extend_grid(source):
    source = jnp.concatenate([source[:, NLON - HALO:], source, source[:, :HALO]], axis=1)
    widths = [(HALO, HALO), (0, 0)] + [(0, 0)] * (source.ndim - 2)
    return jnp.pad(source, widths)

def reference(queries, key_vectors, value_vectors, land_mask, radius, offsets):
    features = queries.shape[2]
    key_extended = extend_grid(key_vectors)
    value_extended = extend_grid(value_vectors)
    land_extended = extend_grid(land_mask)
    zero_index = jnp.zeros((), dtype=jnp.int32)

    def one_tile(tile_at):
        tile_row = (tile_at // N_LON).astype(jnp.int32)
        tile_col = (tile_at % N_LON).astype(jnp.int32)
        row_start = (tile_row * TH).astype(jnp.int32)
        col_start = (tile_col * TW).astype(jnp.int32)
        tile_queries = lax.dynamic_slice(queries, (row_start, col_start, zero_index), (TH, TW, features)).reshape(TH * TW, features)
        near_keys = lax.dynamic_slice(key_extended, (row_start, col_start, zero_index), (TH + 2 * HALO, TW + 2 * HALO, features)).reshape(-1, features)
        near_values = lax.dynamic_slice(value_extended, (row_start, col_start, zero_index), (TH + 2 * HALO, TW + 2 * HALO, features)).reshape(-1, features)
        near_land = lax.dynamic_slice(land_extended, (row_start, col_start), (TH + 2 * HALO, TW + 2 * HALO)).reshape(-1)
        segments = []
        for heading in range(2):
            direction = 1 - 2 * heading
            for level_at in range(LEVELS):
                other_col = ((tile_col + direction * 2 ** (level_at + 1)) % N_LON).astype(jnp.int32)
                far_start = (other_col * TW).astype(jnp.int32)
                tile_keys = lax.dynamic_slice(key_vectors, (row_start, far_start, zero_index), (TH, TW, features)).reshape(-1, features)
                tile_values = lax.dynamic_slice(value_vectors, (row_start, far_start, zero_index), (TH, TW, features)).reshape(-1, features)
                tile_land = lax.dynamic_slice(land_mask, (row_start, far_start), (TH, TW)).reshape(-1)
                segments.append(pick_rows(tile_keys, tile_values, tile_land, offsets[level_at, heading]))
        far_keys = jnp.concatenate([entry[0] for entry in segments], axis=0)
        far_values = jnp.concatenate([entry[1] for entry in segments], axis=0)
        far_land = jnp.concatenate([entry[2] for entry in segments], axis=0)
        return attend(tile_queries, near_keys, near_values, near_land, far_keys, far_values, far_land, radius, TW)
    tiles = lax.map(one_tile, jnp.arange(N_LAT * N_LON, dtype=jnp.int32))
    return tiles.reshape(N_LAT, N_LON, TH, TW, features).transpose(0, 2, 1, 3, 4).reshape(NLAT, NLON, features)
```

```python
import functools

import jax
import jax.numpy as jnp
from jax import lax
from jax.experimental import pallas as pl
from jax.experimental.pallas import tpu as pltpu
from jax.sharding import PartitionSpec as P

TH = 8
TW = 16
TOKENS = TH * TW
HALO = 4
RATE = 4
LEVELS = 2
HEADS = 16
D = 1024
HEAD = D // HEADS
LANES = 128
PAIRS = D // LANES
ROWS = TOKENS // RATE
SIDE = TH * HALO
EDGE = TW * HALO
FLAGS = 8


def iota(shape, dim):
    return lax.broadcasted_iota(jnp.int32, shape, dim)


def land_line(land):
    spread = (iota((TW, TOKENS), 1) % TW == iota((TW, TOKENS), 0)).astype(jnp.float32)
    wide = jnp.dot(land.astype(jnp.float32), spread, preferred_element_type=jnp.float32)
    own = iota((TH, TOKENS), 1) // TW == iota((TH, TOKENS), 0)
    line = jnp.sum(jnp.where(own, wide, 0.0), axis=0, keepdims=True)
    return jnp.broadcast_to(line, (TH, TOKENS))


def flags_tile(line):
    return jnp.concatenate([line, jnp.zeros((FLAGS, D - TOKENS), jnp.float32)], axis=1)


def side_rows(source, start, count, first_row, to_right):
    low = iota((TH, D), 0) < HALO
    found = []
    for r in range(0, count, 2):
        at = start + (first_row + r) * TW + (TW - TH if to_right else 0)
        even, odd = source[pl.ds(at, TH), :], source[pl.ds(at + TW, TH), :]
        if to_right:
            found.append(jnp.where(low, pltpu.roll(even, HALO, 0), odd))
        else:
            found.append(jnp.where(low, even, pltpu.roll(odd, HALO, 0)))
    return jnp.concatenate(found, axis=0)


def dilated_rows(source, at):
    quarter = iota((8, LANES), 0) % RATE
    found = [[] for _ in range(RATE)]
    for g in range(ROWS // 8):
        tiles = [source[pl.ds((g * RATE + i) * 8, 8), at] for i in range(RATE)]
        turned = [[t] + [pltpu.roll(t, d, 0) for d in range(1, RATE)] for t in tiles]
        for o in range(RATE):
            rows = turned[0][-o % RATE]
            for i in range(1, RATE):
                rows = jnp.where(quarter == i, turned[i][(i - o) % RATE], rows)
            found[o].append(rows)
    return [jnp.concatenate(rows, axis=0) for rows in found]


def far_token(n, o):
    i = n % RATE
    half = (n % 8) // RATE
    half = jnp.where(i < o, 1 - half, half)
    return (n // 8 * RATE + i) * 8 + o + RATE * half


def pack_kernel(offsets, k, v, land, up, down, left, right, far0, far1, far2, far3):
    line = flags_tile(land_line(land[...]))
    for part, source in enumerate((k, v)):
        down[pl.ds(part * EDGE, EDGE), :] = source[pl.ds(TOKENS - EDGE, EDGE), :]
        up[pl.ds(part * EDGE, EDGE), :] = source[pl.ds(0, EDGE), :]
        right[pl.ds(part * SIDE, SIDE), :] = side_rows(source, 0, TH, 0, True)
        left[pl.ds(part * SIDE, SIDE), :] = side_rows(source, 0, TH, 0, False)
    up[pl.ds(2 * EDGE, FLAGS), :] = line
    down[pl.ds(2 * EDGE, FLAGS), :] = line
    left[pl.ds(2 * SIDE, FLAGS), :] = line
    right[pl.ds(2 * SIDE, FLAGS), :] = line
    first = iota((ROWS, LANES), 1) < HEAD
    fars = (far0, far1, far2, far3)
    for far in fars:
        far[pl.ds(2 * ROWS, FLAGS), :] = line
    for pair in range(PAIRS):
        at = pl.ds(pair * LANES, LANES)
        for part, source in enumerate((k, v)):
            rows = dilated_rows(source, at)
            for s, far in enumerate(fars):
                want = jnp.where(
                    first,
                    offsets[s // 2, s % 2, 2 * pair],
                    offsets[s // 2, s % 2, 2 * pair + 1],
                )
                picked = rows[0]
                for o in range(1, RATE):
                    picked = jnp.where(want == o, rows[o], picked)
                far[pl.ds(part * ROWS, ROWS), at] = picked


def corner_kernel(above, below, to_right, to_left):
    for part in range(2):
        for target, side in ((to_right, True), (to_left, False)):
            for at, source in ((0, above), (SIDE // 2, below)):
                target[pl.ds(part * SIDE + at, SIDE // 2), :] = side_rows(
                    source, part * EDGE, HALO, 0, side
                )
    high = above[pl.ds(2 * EDGE, FLAGS), :]
    low = below[pl.ds(2 * EDGE, FLAGS), :]
    line = jnp.where(iota((FLAGS, D), 0) == 0, high, low)
    to_right[pl.ds(2 * SIDE, FLAGS), :] = line
    to_left[pl.ds(2 * SIDE, FLAGS), :] = line


def split2(x):
    high = x.astype(jnp.bfloat16)
    low = (x - high.astype(jnp.float32)).astype(jnp.bfloat16)
    return high, low


def split3(x):
    high = x.astype(jnp.bfloat16)
    rest = x - high.astype(jnp.float32)
    mid = rest.astype(jnp.bfloat16)
    low = (rest - mid.astype(jnp.float32)).astype(jnp.bfloat16)
    return high, mid, low


def reach_tables(land, above, below, from_left, from_right, corner_left, corner_right):
    shape = (TOKENS, LANES)
    query_row, query_col = iota(shape, 0) // TW, iota(shape, 0) % TW
    lane = iota(shape, 1)

    def spacing(row, col):
        return jnp.maximum(jnp.abs(query_row - row), jnp.abs(query_col - col))

    def kept(gap, flags):
        return jnp.where((flags > 0.5) | (gap == 0), gap, 99)

    own = kept(spacing(lane // TW, lane % TW), land_line(land[...])[0:1])
    edge_row = jnp.where(lane < EDGE, TH + lane // TW, lane // TW - TH)
    edge_flags = jnp.where(
        iota((1, LANES), 1) < EDGE,
        below[pl.ds(2 * EDGE, 1), 0:LANES],
        above[pl.ds(2 * EDGE, 1), 0:LANES],
    )
    edge = kept(spacing(edge_row, lane % TW), edge_flags)

    group, r, j = lane // SIDE, (lane % SIDE) // HALO, lane % HALO
    side_row = jnp.where(group < 2, r, jnp.where(r < HALO, r - HALO, r + HALO))
    side_col = jnp.where(group % 2 == 0, j - HALO, TW + j)
    lines = jnp.concatenate(
        [
            from_left[pl.ds(2 * SIDE, 1), 0:LANES],
            from_right[pl.ds(2 * SIDE, 1), 0:LANES],
            corner_left[pl.ds(2 * SIDE, 2), 0:LANES],
            corner_right[pl.ds(2 * SIDE, 2), 0:LANES],
            jnp.zeros((2, LANES), jnp.float32),
        ],
        axis=0,
    )
    square = (LANES, LANES)
    lane = iota(square, 1)
    group, r, j = lane // SIDE, (lane % SIDE) // HALO, lane % HALO
    source_row = jnp.where(group < 2, r, (r + HALO) % TH)
    source = source_row * TW + j + jnp.where(group % 2 == 0, TW - HALO, 0)
    pick = (iota(square, 0) == source).astype(jnp.float32)
    picked = jnp.dot(lines, pick, preferred_element_type=jnp.float32)
    lane = iota((8, LANES), 1)
    group, r = lane // SIDE, (lane % SIDE) // HALO
    line_at = jnp.where(group < 2, group, 2 * group - 2 + r // HALO)
    side_flags = jnp.sum(
        jnp.where(iota((8, LANES), 0) == line_at, picked, 0.0), axis=0, keepdims=True
    )
    side = kept(spacing(side_row, side_col), side_flags)
    return own, edge, side


def far_lines(fars):
    lines = jnp.concatenate(
        [far[pl.ds(2 * ROWS, 1), 0:LANES] for far in fars] + [jnp.zeros((4, LANES), jnp.float32)],
        axis=0,
    )
    square = (LANES, LANES)
    found = []
    for o in range(RATE):
        pick = (iota(square, 0) == far_token(iota(square, 1) % ROWS, o)).astype(jnp.float32)
        picked = jnp.dot(lines, pick, preferred_element_type=jnp.float32)
        chosen = iota((8, LANES), 0) == iota((8, LANES), 1) // ROWS
        found.append(jnp.sum(jnp.where(chosen, picked, 0.0), axis=0, keepdims=True))
    return found


def attend_kernel(
    offsets, radius, q, k, v, land, above, below, from_left, from_right, corner_left,
    corner_right, far0, far1, far2, far3, out, reach,
):
    fars = (far0, far1, far2, far3)
    own, edge, side = reach_tables(
        land, above, below, from_left, from_right, corner_left, corner_right
    )
    reach[:, 0:LANES] = own
    reach[:, LANES : 2 * LANES] = edge
    reach[:, 2 * LANES : 3 * LANES] = side
    lines = far_lines(fars)
    group = iota((1, LANES), 1) // ROWS

    def gather(part, at):
        pieces = [(k, v)[part][:, at]]
        pieces += [below[pl.ds(part * EDGE, EDGE), at], above[pl.ds(part * EDGE, EDGE), at]]
        for source in (from_left, from_right, corner_left, corner_right):
            pieces.append(source[pl.ds(part * SIDE, SIDE), at])
        for source in fars:
            pieces.append(source[pl.ds(part * ROWS, ROWS), at])
        return jnp.concatenate(pieces, axis=0)

    def one_pair(pair, carry):
        at = pl.ds(pl.multiple_of(pair * LANES, LANES), LANES)
        k1, k2, k3 = split3(gather(0, at))
        v1, v2 = split2(gather(1, at))
        query = q[:, at] * 0.125
        first = iota((TOKENS, LANES), 1) < HEAD
        query = jnp.concatenate(
            [jnp.where(first, query, 0.0), jnp.where(first, 0.0, query)], axis=0
        )
        q1, q2, q3 = split3(query)
        lhs = jnp.concatenate([q1, q1, q2, q2, q1, q3], axis=1)
        rhs = jnp.concatenate([k1, k2, k1, k2, k3, k1], axis=1)
        score = lax.dot_general(
            lhs, rhs, (((1,), (1,)), ((), ())), preferred_element_type=jnp.float32
        )
        weights, totals = [], []
        for which in range(2):
            head = 2 * pair + which
            mine = score[which * TOKENS : (which + 1) * TOKENS]
            near = jnp.where(reach[...] <= radius[head], mine[:, 0 : 3 * LANES], -jnp.inf)
            want = jnp.where(
                group < 2,
                jnp.where(group == 0, offsets[0, 0, head], offsets[0, 1, head]),
                jnp.where(group == 2, offsets[1, 0, head], offsets[1, 1, head]),
            )
            flags = lines[0]
            for o in range(1, RATE):
                flags = jnp.where(want == o, lines[o], flags)
            far = jnp.where(flags > 0.5, mine[:, 3 * LANES :], -jnp.inf)
            masked = jnp.concatenate([near, far], axis=1)
            top = jnp.max(masked, axis=1, keepdims=True)
            weight = jnp.exp(masked - top)
            totals.append(jnp.sum(weight, axis=1, keepdims=True))
            weights.append(weight)
        p1, p2 = split2(jnp.concatenate(weights, axis=0))
        mixed = jnp.dot(
            p1, jnp.concatenate([v1, v2], axis=1), preferred_element_type=jnp.float32
        )
        rest = jnp.dot(p2, v1, preferred_element_type=jnp.float32)
        mixed = mixed[:, 0:LANES] + mixed[:, LANES:] + rest
        out[:, at] = jnp.where(first, mixed[:TOKENS] / totals[0], mixed[TOKENS:] / totals[1])
        return carry

    lax.fori_loop(0, PAIRS, one_pair, 0)


def shifted(value, axis, steps, periodic=True):
    count = lax.axis_size(axis)
    pairs = [
        (source, (source + steps) % count)
        for source in range(count)
        if periodic or 0 <= source + steps < count
    ]
    return lax.ppermute(value, axis, pairs)


def vmem(count):
    return [pl.BlockSpec(memory_space=pltpu.VMEM)] * count


def smem(count):
    return [pl.BlockSpec(memory_space=pltpu.SMEM)] * count


def payload(rows):
    return jax.ShapeDtypeStruct((rows + FLAGS, D), jnp.float32)


def local(queries, key_vectors, value_vectors, land_mask, radius, offsets):
    k = key_vectors.reshape(TOKENS, D)
    v = value_vectors.reshape(TOKENS, D)
    up, down, left, right, *fars = pl.pallas_call(
        pack_kernel,
        out_shape=[payload(2 * EDGE)] * 2 + [payload(2 * SIDE)] * 2 + [payload(2 * ROWS)] * 4,
        in_specs=smem(1) + vmem(3),
        out_specs=vmem(8),
        cost_estimate=pl.CostEstimate(flops=1 << 20, bytes_accessed=4 << 20, transcendentals=0),
        name="pack",
    )(offsets, k, v, land_mask)
    above = shifted(down, "lat", 1, False)
    below = shifted(up, "lat", -1, False)
    from_left = shifted(right, "lon", 1)
    from_right = shifted(left, "lon", -1)
    arrived = []
    for s in range(4):
        level, heading = s // 2, s % 2
        distance = (1 - 2 * heading) * 2 ** (level + 1)
        arrived.append(shifted(fars[s], "lon", -distance))
    to_right, to_left = pl.pallas_call(
        corner_kernel,
        out_shape=[payload(2 * SIDE)] * 2,
        in_specs=vmem(2),
        out_specs=vmem(2),
        cost_estimate=pl.CostEstimate(flops=1 << 16, bytes_accessed=2 << 20, transcendentals=0),
        name="corners",
    )(above, below)
    corner_left = shifted(to_right, "lon", 1)
    corner_right = shifted(to_left, "lon", -1)
    result = pl.pallas_call(
        attend_kernel,
        out_shape=jax.ShapeDtypeStruct((TOKENS, D), jnp.float32),
        in_specs=smem(2) + vmem(14),
        out_specs=vmem(1)[0],
        scratch_shapes=[pltpu.VMEM((TOKENS, 3 * LANES), jnp.int32)],
        compiler_params=pltpu.CompilerParams(vmem_limit_bytes=32 << 20),
        cost_estimate=pl.CostEstimate(
            flops=1 << 30, bytes_accessed=6 << 20, transcendentals=1 << 20
        ),
        name="attend",
    )(
        offsets, radius, queries.reshape(TOKENS, D), k, v, land_mask, above, below,
        from_left, from_right, corner_left, corner_right, *arrived,
    )
    return result.reshape(TH, TW, D)


def solution(mesh):
    tile = P("lat", "lon", None)
    in_specs = (tile, tile, tile, P("lat", "lon"), P(), P())
    return jax.shard_map(local, mesh=mesh, in_specs=in_specs, out_specs=tile, check_vma=False)
```

```python
import functools

import jax
import jax.numpy as jnp
from jax import lax
from jax.experimental import pallas as pl
from jax.experimental.pallas import tpu as pltpu
from jax.sharding import PartitionSpec as P

TH = 8
TW = 16
TOKENS = TH * TW
HALO = 4
RATE = 4
LEVELS = 2
HEADS = 16
D = 1024
HEAD = D // HEADS
LANES = 128
PAIRS = D // LANES
ROWS = TOKENS // RATE
SIDE = TH * HALO
EDGE = TW * HALO
FLAGS = 8


def iota(shape, dim):
    return lax.broadcasted_iota(jnp.int32, shape, dim)


def land_line(land):
    spread = (iota((TW, TOKENS), 1) % TW == iota((TW, TOKENS), 0)).astype(jnp.float32)
    wide = jnp.dot(land.astype(jnp.float32), spread, preferred_element_type=jnp.float32)
    own = iota((TH, TOKENS), 1) // TW == iota((TH, TOKENS), 0)
    line = jnp.sum(jnp.where(own, wide, 0.0), axis=0, keepdims=True)
    return jnp.broadcast_to(line, (TH, TOKENS))


def flags_tile(line):
    return jnp.concatenate([line, jnp.zeros((FLAGS, D - TOKENS), jnp.float32)], axis=1)


def side_rows(source, start, count, to_right):
    low = iota((TH, D), 0) < HALO
    found = []
    for r in range(0, count, 2):
        at = start + r * TW + (TW - TH if to_right else 0)
        even, odd = source[pl.ds(at, TH), :], source[pl.ds(at + TW, TH), :]
        if to_right:
            found.append(jnp.where(low, pltpu.roll(even, HALO, 0), odd))
        else:
            found.append(jnp.where(low, even, pltpu.roll(odd, HALO, 0)))
    return jnp.concatenate(found, axis=0)


def dilated_rows(source, at):
    quarter = iota((8, LANES), 0) % RATE
    found = [[] for _ in range(RATE)]
    for g in range(ROWS // 8):
        tiles = [source[pl.ds((g * RATE + i) * 8, 8), at] for i in range(RATE)]
        turned = [[t] + [pltpu.roll(t, d, 0) for d in range(1, RATE)] for t in tiles]
        for o in range(RATE):
            rows = turned[0][-o % RATE]
            for i in range(1, RATE):
                rows = jnp.where(quarter == i, turned[i][(i - o) % RATE], rows)
            found[o].append(rows)
    return [jnp.concatenate(rows, axis=0) for rows in found]


def far_token(n, o):
    i = n % RATE
    half = (n % 8) // RATE
    half = jnp.where(i < o, 1 - half, half)
    return (n // 8 * RATE + i) * 8 + o + RATE * half


def edge_kernel(k, v, land, up, down):
    line = flags_tile(land_line(land[...]))
    for part, source in enumerate((k, v)):
        down[pl.ds(part * EDGE, EDGE), :] = source[pl.ds(TOKENS - EDGE, EDGE), :]
        up[pl.ds(part * EDGE, EDGE), :] = source[pl.ds(0, EDGE), :]
    up[pl.ds(2 * EDGE, FLAGS), :] = line
    down[pl.ds(2 * EDGE, FLAGS), :] = line


def far_kernel(offsets, k, v, land, far0, far1, far2, far3):
    line = flags_tile(land_line(land[...]))
    first = iota((ROWS, LANES), 1) < HEAD
    fars = (far0, far1, far2, far3)
    for far in fars:
        far[pl.ds(2 * ROWS, FLAGS), :] = line
    for pair in range(PAIRS):
        at = pl.ds(pair * LANES, LANES)
        for part, source in enumerate((k, v)):
            rows = dilated_rows(source, at)
            for s, far in enumerate(fars):
                want = jnp.where(
                    first,
                    offsets[s // 2, s % 2, 2 * pair],
                    offsets[s // 2, s % 2, 2 * pair + 1],
                )
                picked = rows[0]
                for o in range(1, RATE):
                    picked = jnp.where(want == o, rows[o], picked)
                far[pl.ds(part * ROWS, ROWS), at] = picked


def side_kernel(k, v, land, above, below, to_right, to_left):
    for part, own in enumerate((k, v)):
        for target, right in ((to_right, True), (to_left, False)):
            at = 2 * part * SIDE
            target[pl.ds(at, SIDE), :] = side_rows(own, 0, TH, right)
            target[pl.ds(at + SIDE, SIDE // 2), :] = side_rows(above, part * EDGE, HALO, right)
            target[pl.ds(at + 3 * SIDE // 2, SIDE // 2), :] = side_rows(
                below, part * EDGE, HALO, right
            )
    row = iota((FLAGS, D), 0)
    high = above[pl.ds(2 * EDGE, FLAGS), :]
    low = below[pl.ds(2 * EDGE, FLAGS), :]
    own = flags_tile(land_line(land[...]))
    line = jnp.where(row == 0, own, jnp.where(row == 1, high, low))
    to_right[pl.ds(4 * SIDE, FLAGS), :] = line
    to_left[pl.ds(4 * SIDE, FLAGS), :] = line


def split2(x):
    high = x.astype(jnp.bfloat16)
    low = (x - high.astype(jnp.float32)).astype(jnp.bfloat16)
    return high, low


def split3(x):
    high = x.astype(jnp.bfloat16)
    rest = x - high.astype(jnp.float32)
    mid = rest.astype(jnp.bfloat16)
    low = (rest - mid.astype(jnp.float32)).astype(jnp.bfloat16)
    return high, mid, low


def spacing(row, col):
    query = iota((TOKENS, LANES), 0)
    return jnp.maximum(jnp.abs(query // TW - row), jnp.abs(query % TW - col))


def kept(gap, flags):
    return jnp.where((flags > 0.5) | (gap == 0), gap, 99)


def own_reach(land):
    lane = iota((TOKENS, LANES), 1)
    return kept(spacing(lane // TW, lane % TW), land_line(land[...])[0:1])


def edge_reach(above, below):
    lane = iota((TOKENS, LANES), 1)
    row = jnp.where(lane < EDGE, TH + lane // TW, lane // TW - TH)
    flags = jnp.where(
        iota((1, LANES), 1) < EDGE,
        below[pl.ds(2 * EDGE, 1), 0:LANES],
        above[pl.ds(2 * EDGE, 1), 0:LANES],
    )
    return kept(spacing(row, lane % TW), flags)


def side_reach(from_left, from_right):
    lines = jnp.concatenate(
        [
            from_left[pl.ds(4 * SIDE, 3), 0:LANES],
            from_right[pl.ds(4 * SIDE, 3), 0:LANES],
            jnp.zeros((2, LANES), jnp.float32),
        ],
        axis=0,
    )

    def places(shape):
        lane = iota(shape, 1)
        return lane // (2 * SIDE), lane // SIDE % 2, lane % SIDE // HALO, lane % HALO

    square = (LANES, LANES)
    right, corner, r, j = places(square)
    row = jnp.where(corner == 0, r, jnp.where(r < HALO, r - HALO, r + HALO))
    gap = spacing(row, jnp.where(right == 0, j - HALO, TW + j))
    source = row % TH * TW + j + jnp.where(right == 0, TW - HALO, 0)
    pick = (iota(square, 0) == source).astype(jnp.float32)
    picked = jnp.dot(lines, pick, preferred_element_type=jnp.float32)
    right, corner, r, j = places((8, LANES))
    line = 3 * right + jnp.where(corner == 0, 0, 1 + r // HALO)
    flags = jnp.sum(jnp.where(iota((8, LANES), 0) == line, picked, 0.0), axis=0, keepdims=True)
    return kept(gap, flags)


def far_lines(fars):
    lines = jnp.concatenate(
        [far[pl.ds(2 * ROWS, 1), 0:LANES] for far in fars] + [jnp.zeros((4, LANES), jnp.float32)],
        axis=0,
    )
    square = (LANES, LANES)
    found = []
    for o in range(RATE):
        pick = (iota(square, 0) == far_token(iota(square, 1) % ROWS, o)).astype(jnp.float32)
        picked = jnp.dot(lines, pick, preferred_element_type=jnp.float32)
        chosen = iota((8, LANES), 0) == iota((8, LANES), 1) // ROWS
        found.append(jnp.sum(jnp.where(chosen, picked, 0.0), axis=0, keepdims=True))
    return found


def twice(x):
    first = iota(x.shape, 1) < HEAD
    return jnp.concatenate([jnp.where(first, x, 0.0), jnp.where(first, 0.0, x)], axis=0)


def once(x):
    return jnp.where(iota((TOKENS, LANES), 1) < HEAD, x[:TOKENS], x[TOKENS:])


def scores(query, key):
    q1, q2, q3 = split3(query)
    k1, k2, k3 = split3(key)
    return lax.dot_general(
        jnp.concatenate([q1, q1, q2, q2, q1, q3], axis=1),
        jnp.concatenate([k1, k2, k1, k2, k3, k1], axis=1),
        (((1,), (1,)), ((), ())),
        preferred_element_type=jnp.float32,
    )


def mixture(masked, top, value):
    weight = jnp.exp(masked - top)
    total = jnp.sum(weight, axis=1, keepdims=True)
    p1, p2 = split2(weight)
    v1, v2 = split2(value)
    mixed = jnp.dot(p1, jnp.concatenate([v1, v2], axis=1), preferred_element_type=jnp.float32)
    rest = jnp.dot(p2, v1, preferred_element_type=jnp.float32)
    return once(mixed[:, :LANES] + mixed[:, LANES:] + rest), once(
        jnp.broadcast_to(total, (2 * TOKENS, LANES))
    )


def pair_loop(body):
    def step(pair, carry):
        body(pair, pl.ds(pl.multiple_of(pair * LANES, LANES), LANES))
        return carry

    lax.fori_loop(0, PAIRS, step, 0)


def first_kernel(
    offsets, radius, q, k, v, land, above, below, far0, far1, far2, far3, mixed, total, peak, reach
):
    fars = (far0, far1, far2, far3)
    reach[:, 0:LANES] = own_reach(land)
    reach[:, LANES : 2 * LANES] = edge_reach(above, below)
    lines = far_lines(fars)
    group = iota((1, LANES), 1) // ROWS

    def gather(part, at):
        pieces = [(k, v)[part][:, at]]
        pieces += [below[pl.ds(part * EDGE, EDGE), at], above[pl.ds(part * EDGE, EDGE), at]]
        pieces += [source[pl.ds(part * ROWS, ROWS), at] for source in fars]
        return jnp.concatenate(pieces, axis=0)

    def body(pair, at):
        score = scores(twice(q[:, at] * 0.125), gather(0, at))
        both = []
        for which in range(2):
            head = 2 * pair + which
            mine = score[which * TOKENS : (which + 1) * TOKENS]
            near = jnp.where(reach[...] <= radius[head], mine[:, 0 : 2 * LANES], -jnp.inf)
            want = jnp.where(
                group < 2,
                jnp.where(group == 0, offsets[0, 0, head], offsets[0, 1, head]),
                jnp.where(group == 2, offsets[1, 0, head], offsets[1, 1, head]),
            )
            flags = lines[0]
            for o in range(1, RATE):
                flags = jnp.where(want == o, lines[o], flags)
            far = jnp.where(flags > 0.5, mine[:, 2 * LANES :], -jnp.inf)
            both.append(jnp.concatenate([near, far], axis=1))
        masked = jnp.concatenate(both, axis=0)
        top = jnp.max(masked, axis=1, keepdims=True)
        peak[:, at] = once(jnp.broadcast_to(top, (2 * TOKENS, LANES)))
        mixed[:, at], total[:, at] = mixture(masked, top, gather(1, at))

    pair_loop(body)


def second_kernel(radius, q, from_left, from_right, mixed, total, peak, out, reach):
    reach[...] = side_reach(from_left, from_right)

    def gather(part, at):
        return jnp.concatenate(
            [source[pl.ds(2 * part * SIDE, 2 * SIDE), at] for source in (from_left, from_right)],
            axis=0,
        )

    def body(pair, at):
        score = scores(twice(q[:, at] * 0.125), gather(0, at))
        both = []
        for which in range(2):
            mine = score[which * TOKENS : (which + 1) * TOKENS]
            both.append(jnp.where(reach[...] <= radius[2 * pair + which], mine, -jnp.inf))
        masked = jnp.concatenate(both, axis=0)
        before = peak[:, at]
        first = iota((TOKENS, LANES), 1) < HEAD
        old = jnp.concatenate(
            [
                jnp.max(jnp.where(first, before, -jnp.inf), axis=1, keepdims=True),
                jnp.max(jnp.where(first, -jnp.inf, before), axis=1, keepdims=True),
            ],
            axis=0,
        )
        top = jnp.maximum(jnp.max(masked, axis=1, keepdims=True), old)
        mix, weight = mixture(masked, top, gather(1, at))
        shrink = jnp.exp(before - once(jnp.broadcast_to(top, (2 * TOKENS, LANES))))
        out[:, at] = (mixed[:, at] * shrink + mix) / (total[:, at] * shrink + weight)

    pair_loop(body)


def shifted(value, axis, steps, periodic=True):
    count = lax.axis_size(axis)
    pairs = [
        (source, (source + steps) % count)
        for source in range(count)
        if periodic or 0 <= source + steps < count
    ]
    return lax.ppermute(value, axis, pairs)


def vmem(count):
    return [pl.BlockSpec(memory_space=pltpu.VMEM)] * count


def smem(count):
    return [pl.BlockSpec(memory_space=pltpu.SMEM)] * count


def payload(rows):
    return jax.ShapeDtypeStruct((rows + FLAGS, D), jnp.float32)


def call(kernel, name, outs, smems, vmems, flops, moved, scratch=(), limit=16):
    return pl.pallas_call(
        kernel,
        out_shape=outs,
        in_specs=smem(smems) + vmem(vmems),
        out_specs=vmem(len(outs)),
        scratch_shapes=list(scratch),
        compiler_params=pltpu.CompilerParams(vmem_limit_bytes=limit << 20),
        cost_estimate=pl.CostEstimate(
            flops=flops, bytes_accessed=moved << 20, transcendentals=0
        ),
        name=name,
    )


def local(queries, key_vectors, value_vectors, land_mask, radius, offsets):
    q = queries.reshape(TOKENS, D)
    k = key_vectors.reshape(TOKENS, D)
    v = value_vectors.reshape(TOKENS, D)
    tile = jax.ShapeDtypeStruct((TOKENS, D), jnp.float32)
    up, down = call(edge_kernel, "edge", [payload(2 * EDGE)] * 2, 0, 3, 1 << 16, 2)(
        k, v, land_mask
    )
    above = shifted(down, "lat", 1, False)
    below = shifted(up, "lat", -1, False)
    fars = call(far_kernel, "far", [payload(2 * ROWS)] * 4, 1, 3, 1 << 20, 2)(
        offsets, k, v, land_mask
    )
    fars, arrived = list(fars), [None] * 4
    for s in (2, 3, 0, 1):
        level, heading = s // 2, s % 2
        distance = (1 - 2 * heading) * 2 ** (level + 1)
        if s == 1:
            arrived[2], fars[1] = lax.optimization_barrier((arrived[2], fars[1]))
        arrived[s] = shifted(fars[s], "lon", -distance)
    to_right, to_left = call(
        side_kernel, "side", [payload(4 * SIDE)] * 2, 0, 5, 1 << 33, 3
    )(k, v, land_mask, above, below)
    from_left = shifted(to_right, "lon", 1)
    from_right = shifted(to_left, "lon", -1)
    partial = call(
        first_kernel, "first", [tile] * 3, 2, 10, 1 << 34, 6,
        [pltpu.VMEM((TOKENS, 2 * LANES), jnp.int32)], 24,
    )(offsets, radius, q, k, v, land_mask, above, below, *arrived)
    [result] = call(
        second_kernel, "second", [tile], 1, 6, 1 << 28, 4,
        [pltpu.VMEM((TOKENS, LANES), jnp.int32)],
    )(radius, q, from_left, from_right, *partial)
    return result.reshape(TH, TW, D)


def solution(mesh):
    tile = P("lat", "lon", None)
    in_specs = (tile, tile, tile, P("lat", "lon"), P(), P())
    return jax.shard_map(local, mesh=mesh, in_specs=in_specs, out_specs=tile, check_vma=False)
```

```python
import functools

import jax
import jax.numpy as jnp
from jax import lax
from jax.experimental import pallas as pl
from jax.experimental.pallas import tpu as pltpu
from jax.sharding import PartitionSpec as P

TH = 8
TW = 16
TOKENS = TH * TW
HALO = 4
RATE = 4
LEVELS = 2
HEADS = 16
D = 1024
HEAD = D // HEADS
LANES = 128
PAIRS = D // LANES
ROWS = TOKENS // RATE
SIDE = TH * HALO
EDGE = TW * HALO
FLAGS = 8


def iota(shape, dim):
    return lax.broadcasted_iota(jnp.int32, shape, dim)


def land_line(land):
    spread = (iota((TW, TOKENS), 1) % TW == iota((TW, TOKENS), 0)).astype(jnp.float32)
    wide = jnp.dot(land.astype(jnp.float32), spread, preferred_element_type=jnp.float32)
    own = iota((TH, TOKENS), 1) // TW == iota((TH, TOKENS), 0)
    line = jnp.sum(jnp.where(own, wide, 0.0), axis=0, keepdims=True)
    return jnp.broadcast_to(line, (TH, TOKENS))


def block(rows, pair, part):
    return pl.ds((2 * pair + part) * rows, rows)


def flags_at(rows, count=FLAGS):
    return pl.ds(2 * PAIRS * rows, count)


def side_rows(read, to_right, count):
    low = iota((8, LANES), 0) < HALO
    found = []
    for r in range(0, count, 2):
        at = r * TW + (TW - TH if to_right else 0)
        even, odd = read(at), read(at + TW)
        if to_right:
            found.append(jnp.where(low, pltpu.roll(even, HALO, 0), odd))
        else:
            found.append(jnp.where(low, even, pltpu.roll(odd, HALO, 0)))
    return found


def dilated_rows(source, at):
    quarter = iota((8, LANES), 0) % RATE
    found = [[] for _ in range(RATE)]
    for g in range(ROWS // 8):
        tiles = [source[pl.ds((g * RATE + i) * 8, 8), at] for i in range(RATE)]
        turned = [[t] + [pltpu.roll(t, d, 0) for d in range(1, RATE)] for t in tiles]
        for o in range(RATE):
            rows = turned[0][-o % RATE]
            for i in range(1, RATE):
                rows = jnp.where(quarter == i, turned[i][(i - o) % RATE], rows)
            found[o].append(rows)
    return [jnp.concatenate(rows, axis=0) for rows in found]


def far_token(n, o):
    i = n % RATE
    half = (n % 8) // RATE
    half = jnp.where(i < o, 1 - half, half)
    return (n // 8 * RATE + i) * 8 + o + RATE * half


def edge_kernel(k, v, land, up, down, flags, sems, flags_sem):
    fetch = pltpu.make_async_copy(land, flags, flags_sem)
    fetch.start()
    copies = []
    for pair in range(PAIRS):
        for part, source in enumerate((k, v)):
            for which, (target, start) in enumerate(((up, 0), (down, TOKENS - EDGE))):
                copies.append(
                    pltpu.make_async_copy(
                        source.at[pl.ds(start, EDGE), pl.ds(pair * LANES, LANES)],
                        target.at[block(EDGE, pair, part), :],
                        sems.at[(2 * pair + part) * 2 + which],
                    )
                )
                copies[-1].start()
    fetch.wait()
    line = land_line(flags[...])
    up[flags_at(EDGE), :] = line
    down[flags_at(EDGE), :] = line
    for copy in copies:
        copy.wait()


def far_kernel(offsets, k, v, land, far0, far1, far2, far3):
    line = land_line(land[...])
    first = iota((ROWS, LANES), 1) < HEAD
    fars = (far0, far1, far2, far3)
    for far in fars:
        far[flags_at(ROWS), :] = line
    for pair in range(PAIRS):
        at = pl.ds(pair * LANES, LANES)
        for part, source in enumerate((k, v)):
            rows = dilated_rows(source, at)
            for s, far in enumerate(fars):
                want = jnp.where(
                    first,
                    offsets[s // 2, s % 2, 2 * pair],
                    offsets[s // 2, s % 2, 2 * pair + 1],
                )
                picked = rows[0]
                for o in range(1, RATE):
                    picked = jnp.where(want == o, rows[o], picked)
                far[block(ROWS, pair, part), :] = picked


def side_kernel(k, v, land, above, below, to_right, to_left):
    for pair in range(PAIRS):
        at = pl.ds(pair * LANES, LANES)
        for part, own in enumerate((k, v)):
            start = (2 * pair + part) * EDGE
            for target, right in ((to_right, True), (to_left, False)):
                rows = side_rows(lambda row: own[pl.ds(row, 8), at], right, TH)
                for source in (above, below):
                    rows += side_rows(lambda row: source[pl.ds(start + row, 8), :], right, HALO)
                target[block(2 * SIDE, pair, part), :] = jnp.concatenate(rows, axis=0)
    row = iota((FLAGS, LANES), 0)
    near = land_line(land[...])
    line = jnp.where(
        row == 0, near, jnp.where(row == 1, above[flags_at(EDGE), :], below[flags_at(EDGE), :])
    )
    to_right[flags_at(2 * SIDE), :] = line
    to_left[flags_at(2 * SIDE), :] = line


def split2(x):
    high = x.astype(jnp.bfloat16)
    low = (x - high.astype(jnp.float32)).astype(jnp.bfloat16)
    return high, low


def split3(x):
    high = x.astype(jnp.bfloat16)
    rest = x - high.astype(jnp.float32)
    mid = rest.astype(jnp.bfloat16)
    low = (rest - mid.astype(jnp.float32)).astype(jnp.bfloat16)
    return high, mid, low


def spacing(row, col):
    query = iota(row.shape, 1)
    return jnp.maximum(jnp.abs(query // TW - row), jnp.abs(query % TW - col))


def across(x, y):
    return lax.dot_general(x, y, (((1,), (1,)), ((), ())), preferred_element_type=jnp.float32)


def flag_columns(line, token, lines):
    shape = (line.shape[0], LANES)
    spot = line * LANES + token - iota(shape, 1)
    pick = [(spot == at * LANES).astype(jnp.bfloat16) for at in range(len(lines))]
    rows = [jnp.broadcast_to(row, (LANES, LANES)).astype(jnp.bfloat16) for row in lines]
    return across(jnp.concatenate(pick, axis=1), jnp.concatenate(rows, axis=1))


def reach(row, col, flags):
    gap = spacing(row, col)
    return jnp.where((flags > 0.5) | (gap == 0), gap, 99)


def own_reach(land):
    key = iota((TOKENS, LANES), 0)
    return reach(key // TW, key % TW, flag_columns(key * 0, key, [land_line(land[...])[0:1]]))


def edge_reach(above, below):
    key = iota((2 * EDGE, LANES), 0)
    row = jnp.where(key < EDGE, TH + key // TW, key // TW - TH)
    lines = [source[flags_at(EDGE, 1), :] for source in (below, above)]
    return reach(row, key % TW, flag_columns(key // EDGE, key, lines))


def side_reach(from_left, from_right):
    key = iota((4 * SIDE, LANES), 0)
    right, corner = key // (2 * SIDE), key // SIDE % 2
    r, j = key % SIDE // HALO, key % HALO
    row = jnp.where(corner == 0, r, jnp.where(r < HALO, r - HALO, r + HALO))
    col = jnp.where(right == 0, j - HALO, TW + j)
    token = (row + TH) % TH * TW + (col + TW) % TW
    line = 3 * right + jnp.where(corner == 0, 0, 1 + r // HALO)
    lines = []
    for source in (from_left, from_right):
        found = source[flags_at(2 * SIDE), :]
        lines += [found[i : i + 1] for i in range(3)]
    return reach(row, col, flag_columns(line, token, lines))


def far_bias(far):
    key = iota((TOKENS, LANES), 0)
    token = far_token(key % ROWS, key // ROWS)
    flags = flag_columns(key * 0, token, [far[flags_at(ROWS, 1), :]])
    return jnp.where(flags > 0.5, 0.0, -jnp.inf)


def near_bias(bias, at, found):
    for r in range(HALO):
        bias[r, pl.ds(at, found.shape[0]), :] = jnp.where(found <= r + 1, 0.0, -jnp.inf)


def twice(x):
    first = iota(x.shape, 1) < HEAD
    return jnp.concatenate([jnp.where(first, x, 0.0), jnp.where(first, 0.0, x)], axis=0)


def own_columns(x):
    return jnp.concatenate([x[:HEAD, :TOKENS], x[HEAD:, TOKENS:]], axis=0)


def over_features(x):
    return jnp.concatenate(
        [
            jnp.broadcast_to(x[:, :TOKENS], (HEAD, TOKENS)),
            jnp.broadcast_to(x[:, TOKENS:], (HEAD, TOKENS)),
        ],
        axis=0,
    )


def scores(key, query):
    q1, q2, q3 = split3(twice(query * 0.125))
    k1, k2, k3 = split3(key)
    return across(
        jnp.concatenate([k1, k2, k1, k2, k3, k1], axis=1),
        jnp.concatenate([q1, q1, q2, q2, q1, q3], axis=1),
    )


def mixture(weight, value):
    p1, p2 = split2(weight)
    v1, v2 = split2(value)
    eye = (iota((LANES, LANES), 0) == iota((LANES, LANES), 1)).astype(jnp.bfloat16)
    v1 = across(eye, v1).astype(jnp.bfloat16)
    v2 = across(eye, v2).astype(jnp.bfloat16)
    ones = jnp.ones((16, weight.shape[0]), jnp.bfloat16)
    high = jnp.dot(
        jnp.concatenate([v1, v2, ones], axis=0), p1, preferred_element_type=jnp.float32
    )
    low = jnp.dot(jnp.concatenate([v1, ones], axis=0), p2, preferred_element_type=jnp.float32)
    mixed = own_columns(high[:LANES]) + own_columns(high[LANES : 2 * LANES])
    total = high[2 * LANES : 2 * LANES + 1] + low[LANES : LANES + 1]
    return mixed + own_columns(low[:LANES]), total


def first_kernel(
    offsets, radius, q, k, v, land, above, below, far0, far1, far2, far3, mixed, total, peak,
    near, beyond,
):
    fars = (far0, far1, far2, far3)
    near_bias(near, 0, own_reach(land))
    near_bias(near, TOKENS, edge_reach(above, below))
    for s, far in enumerate(fars):
        beyond[s] = far_bias(far)

    def gather(part, pair, at):
        pieces = [(k, v)[part][:, at]]
        pieces += [source[block(EDGE, pair, part), :] for source in (below, above)]
        pieces += [source[block(ROWS, pair, part), :] for source in fars]
        return jnp.concatenate(pieces, axis=0)

    def barrier(pair):
        bias = []
        for head in (2 * pair, 2 * pair + 1):
            rows = [near[radius[head] - 1]]
            for s in range(4):
                start = pl.multiple_of(offsets[s // 2, s % 2, head] * ROWS, ROWS)
                rows.append(beyond[s, pl.ds(start, ROWS), :])
            bias.append(jnp.concatenate(rows, axis=0))
        return jnp.concatenate(bias, axis=1)

    def body(pairs, ats):
        masked = [scores(gather(0, pair, at), q[:, at]) for pair, at in zip(pairs, ats)]
        masked = [x + barrier(pair) for x, pair in zip(masked, pairs)]
        tops = [jnp.max(x, axis=0, keepdims=True) for x in masked]
        weights = [jnp.exp(x - top) for x, top in zip(masked, tops)]
        mixes = [mixture(x, gather(1, *at)) for x, at in zip(weights, zip(pairs, ats))]
        for pair, at, top, (mix, weight) in zip(pairs, ats, tops, mixes):
            mixed[at, :] = mix
            total[pair] = jnp.broadcast_to(weight, (8, 2 * TOKENS))
            peak[pair] = jnp.broadcast_to(top, (8, 2 * TOKENS))

    body(range(PAIRS), [pl.ds(pair * LANES, LANES) for pair in range(PAIRS)])


def second_kernel(radius, q, from_left, from_right, mixed, total, peak, out, near):
    near_bias(near, 0, side_reach(from_left, from_right))

    def gather(part, pair):
        return jnp.concatenate(
            [source[block(2 * SIDE, pair, part), :] for source in (from_left, from_right)], axis=0
        )

    def barrier(pair):
        return jnp.concatenate([near[radius[head] - 1] for head in (2 * pair, 2 * pair + 1)], axis=1)

    def body(pairs, ats):
        masked = [scores(gather(0, pair), q[:, at]) for pair, at in zip(pairs, ats)]
        masked = [x + barrier(pair) for x, pair in zip(masked, pairs)]
        old = [peak[pair][0:1] for pair in pairs]
        tops = [jnp.maximum(jnp.max(x, axis=0, keepdims=True), y) for x, y in zip(masked, old)]
        weights = [jnp.exp(x - top) for x, top in zip(masked, tops)]
        mixes = [mixture(x, gather(1, pair)) for x, pair in zip(weights, pairs)]
        done = []
        for pair, at, top, before, (mix, weight) in zip(pairs, ats, tops, old, mixes):
            shrink = jnp.exp(before - top)
            inverse = 1.0 / (total[pair][0:1] * shrink + weight)
            done.append(
                mixed[at, :] * over_features(shrink * inverse) + mix * over_features(inverse)
            )
        for at, mix in zip(ats, done):
            out[:, at] = mix.T

    body(range(PAIRS), [pl.ds(pair * LANES, LANES) for pair in range(PAIRS)])


def shifted(value, axis, steps, periodic=True):
    count = lax.axis_size(axis)
    pairs = [
        (source, (source + steps) % count)
        for source in range(count)
        if periodic or 0 <= source + steps < count
    ]
    return lax.ppermute(value, axis, pairs)


def vmem(count):
    return [pl.BlockSpec(memory_space=pltpu.VMEM)] * count


def smem(count):
    return [pl.BlockSpec(memory_space=pltpu.SMEM)] * count


def payload(rows):
    return jax.ShapeDtypeStruct((2 * PAIRS * rows + FLAGS, LANES), jnp.float32)


def call(kernel, name, outs, smems, vmems, flops, moved, scratch=(), limit=16):
    return pl.pallas_call(
        kernel,
        out_shape=outs,
        in_specs=smem(smems) + vmem(vmems),
        out_specs=vmem(len(outs)),
        scratch_shapes=list(scratch),
        compiler_params=pltpu.CompilerParams(vmem_limit_bytes=limit << 20),
        cost_estimate=pl.CostEstimate(
            flops=flops, bytes_accessed=moved << 20, transcendentals=0
        ),
        name=name,
    )


def local(queries, key_vectors, value_vectors, land_mask, radius, offsets):
    q = queries.reshape(TOKENS, D)
    k = key_vectors.reshape(TOKENS, D)
    v = value_vectors.reshape(TOKENS, D)
    up, down = pl.pallas_call(
        edge_kernel,
        out_shape=[payload(EDGE)] * 2,
        in_specs=[pl.BlockSpec(memory_space=pltpu.HBM)] * 3,
        out_specs=vmem(2),
        scratch_shapes=[
            pltpu.VMEM((TH, TW), jnp.int32),
            pltpu.SemaphoreType.DMA((4 * PAIRS,)),
            pltpu.SemaphoreType.DMA,
        ],
        compiler_params=pltpu.CompilerParams(vmem_limit_bytes=58 << 20),
        cost_estimate=pl.CostEstimate(flops=1 << 16, bytes_accessed=2 << 20, transcendentals=0),
        name="edge",
    )(k, v, land_mask)
    k, v, land_mask, up, down = lax.optimization_barrier((k, v, land_mask, up, down))
    above = shifted(down, "lat", 1, False)
    below = shifted(up, "lat", -1, False)
    fars = call(far_kernel, "far", [payload(ROWS)] * 4, 1, 3, 1 << 20, 2)(
        offsets, k, v, land_mask
    )
    fars, arrived = list(fars), [None] * 4
    for s in (2, 3, 0, 1):
        level, heading = s // 2, s % 2
        distance = (1 - 2 * heading) * 2 ** (level + 1)
        if s == 1:
            arrived[2], fars[1] = lax.optimization_barrier((arrived[2], fars[1]))
        arrived[s] = shifted(fars[s], "lon", -distance)
    to_right, to_left = call(
        side_kernel, "side", [payload(2 * SIDE)] * 2, 0, 5, 1 << 33, 3
    )(k, v, land_mask, above, below)
    from_left = shifted(to_right, "lon", 1)
    from_right = shifted(to_left, "lon", -1)
    line = jax.ShapeDtypeStruct((PAIRS, 8, 2 * TOKENS), jnp.float32)
    partial = call(
        first_kernel, "first", [jax.ShapeDtypeStruct((D, TOKENS), jnp.float32), line, line],
        2, 10, 1 << 34, 6,
        [
            pltpu.VMEM((HALO, 2 * TOKENS, LANES), jnp.float32),
            pltpu.VMEM((4, TOKENS, LANES), jnp.float32),
        ],
        24,
    )(offsets, radius, q, k, v, land_mask, above, below, *arrived)
    [result] = call(
        second_kernel, "second", [jax.ShapeDtypeStruct((TOKENS, D), jnp.float32)],
        1, 6, 1 << 28, 4, [pltpu.VMEM((HALO, TOKENS, LANES), jnp.float32)],
    )(radius, q, from_left, from_right, *partial)
    return result.reshape(TH, TW, D)


def solution(mesh):
    tile = P("lat", "lon", None)
    in_specs = (tile, tile, tile, P("lat", "lon"), P(), P())
    return jax.shard_map(local, mesh=mesh, in_specs=in_specs, out_specs=tile, check_vma=False)
```

```python
import functools

import jax
import jax.numpy as jnp
from jax import lax
from jax.experimental import pallas as pl
from jax.experimental.pallas import tpu as pltpu
from jax.sharding import PartitionSpec as P

TH = 8
TW = 16
TOKENS = TH * TW
HALO = 4
RATE = 4
LEVELS = 2
HEADS = 16
D = 1024
HEAD = D // HEADS
LANES = 128
PAIRS = D // LANES
ROWS = TOKENS // RATE
SIDE = TH * HALO
EDGE = TW * HALO
FLAGS = 8


def iota(shape, dim):
    return lax.broadcasted_iota(jnp.int32, shape, dim)


def land_line(land):
    spread = (iota((TW, TOKENS), 1) % TW == iota((TW, TOKENS), 0)).astype(jnp.float32)
    wide = jnp.dot(land.astype(jnp.float32), spread, preferred_element_type=jnp.float32)
    own = iota((TH, TOKENS), 1) // TW == iota((TH, TOKENS), 0)
    line = jnp.sum(jnp.where(own, wide, 0.0), axis=0, keepdims=True)
    return jnp.broadcast_to(line, (TH, TOKENS))


def block(rows, pair, part):
    return pl.ds((2 * pair + part) * rows, rows)


def flags_at(rows, count=FLAGS):
    return pl.ds(2 * PAIRS * rows, count)


def side_rows(read, to_right, count):
    low = iota((8, LANES), 0) < HALO
    found = []
    for r in range(0, count, 2):
        at = r * TW + (TW - TH if to_right else 0)
        even, odd = read(at), read(at + TW)
        if to_right:
            found.append(jnp.where(low, pltpu.roll(even, HALO, 0), odd))
        else:
            found.append(jnp.where(low, even, pltpu.roll(odd, HALO, 0)))
    return found


def dilated_rows(source, at):
    quarter = iota((8, LANES), 0) % RATE
    found = [[] for _ in range(RATE)]
    for g in range(ROWS // 8):
        tiles = [source[pl.ds((g * RATE + i) * 8, 8), at] for i in range(RATE)]
        turned = [[t] + [pltpu.roll(t, d, 0) for d in range(1, RATE)] for t in tiles]
        for o in range(RATE):
            rows = turned[0][-o % RATE]
            for i in range(1, RATE):
                rows = jnp.where(quarter == i, turned[i][(i - o) % RATE], rows)
            found[o].append(rows)
    return [jnp.concatenate(rows, axis=0) for rows in found]


def far_token(n, o):
    i = n % RATE
    half = (n % 8) // RATE
    half = jnp.where(i < o, 1 - half, half)
    return (n // 8 * RATE + i) * 8 + o + RATE * half


def edge_kernel(k, v, land, up, down, flags, sems, flags_sem):
    fetch = pltpu.make_async_copy(land, flags, flags_sem)
    fetch.start()
    copies = []
    for pair in range(PAIRS):
        for part, source in enumerate((k, v)):
            for which, (target, start) in enumerate(((up, 0), (down, TOKENS - EDGE))):
                copies.append(
                    pltpu.make_async_copy(
                        source.at[pl.ds(start, EDGE), pl.ds(pair * LANES, LANES)],
                        target.at[block(EDGE, pair, part), :],
                        sems.at[(2 * pair + part) * 2 + which],
                    )
                )
                copies[-1].start()
    fetch.wait()
    line = land_line(flags[...])
    up[flags_at(EDGE), :] = line
    down[flags_at(EDGE), :] = line
    for copy in copies:
        copy.wait()


def far_kernel(offsets, k, v, land, far0, far1, far2, far3):
    line = land_line(land[...])
    first = iota((ROWS, LANES), 1) < HEAD
    fars = (far0, far1, far2, far3)
    for far in fars:
        far[flags_at(ROWS), :] = line
    for pair in range(PAIRS):
        at = pl.ds(pair * LANES, LANES)
        for part, source in enumerate((k, v)):
            rows = dilated_rows(source, at)
            for s, far in enumerate(fars):
                want = jnp.where(
                    first,
                    offsets[s // 2, s % 2, 2 * pair],
                    offsets[s // 2, s % 2, 2 * pair + 1],
                )
                picked = rows[0]
                for o in range(1, RATE):
                    picked = jnp.where(want == o, rows[o], picked)
                far[block(ROWS, pair, part), :] = picked


def side_kernel(k, v, land, above, below, to_right, to_left):
    for pair in range(PAIRS):
        at = pl.ds(pair * LANES, LANES)
        for part, own in enumerate((k, v)):
            start = (2 * pair + part) * EDGE
            for target, right in ((to_right, True), (to_left, False)):
                rows = side_rows(lambda row: own[pl.ds(row, 8), at], right, TH)
                for source in (above, below):
                    rows += side_rows(lambda row: source[pl.ds(start + row, 8), :], right, HALO)
                target[block(2 * SIDE, pair, part), :] = jnp.concatenate(rows, axis=0)
    row = iota((FLAGS, LANES), 0)
    near = land_line(land[...])
    line = jnp.where(
        row == 0, near, jnp.where(row == 1, above[flags_at(EDGE), :], below[flags_at(EDGE), :])
    )
    to_right[flags_at(2 * SIDE), :] = line
    to_left[flags_at(2 * SIDE), :] = line


def split2(x):
    high = x.astype(jnp.bfloat16)
    low = (x - high.astype(jnp.float32)).astype(jnp.bfloat16)
    return high, low


def split3(x):
    high = x.astype(jnp.bfloat16)
    rest = x - high.astype(jnp.float32)
    mid = rest.astype(jnp.bfloat16)
    low = (rest - mid.astype(jnp.float32)).astype(jnp.bfloat16)
    return high, mid, low


def spacing(row, col):
    query = iota(row.shape, 1)
    return jnp.maximum(jnp.abs(query // TW - row), jnp.abs(query % TW - col))


def across(x, y):
    return lax.dot_general(x, y, (((1,), (1,)), ((), ())), preferred_element_type=jnp.float32)


def flag_columns(line, token, lines):
    shape = (line.shape[0], LANES)
    spot = line * LANES + token - iota(shape, 1)
    pick = [(spot == at * LANES).astype(jnp.bfloat16) for at in range(len(lines))]
    rows = [jnp.broadcast_to(row, (LANES, LANES)).astype(jnp.bfloat16) for row in lines]
    return across(jnp.concatenate(pick, axis=1), jnp.concatenate(rows, axis=1))


def reach(row, col, flags):
    gap = spacing(row, col)
    return jnp.where((flags > 0.5) | (gap == 0), gap, 99)


def own_reach(land):
    key = iota((TOKENS, LANES), 0)
    return reach(key // TW, key % TW, flag_columns(key * 0, key, [land_line(land[...])[0:1]]))


def edge_reach(above, below):
    key = iota((2 * EDGE, LANES), 0)
    row = jnp.where(key < EDGE, TH + key // TW, key // TW - TH)
    lines = [source[flags_at(EDGE, 1), :] for source in (below, above)]
    return reach(row, key % TW, flag_columns(key // EDGE, key, lines))


def side_reach(from_left, from_right):
    key = iota((4 * SIDE, LANES), 0)
    right, corner = key // (2 * SIDE), key // SIDE % 2
    r, j = key % SIDE // HALO, key % HALO
    row = jnp.where(corner == 0, r, jnp.where(r < HALO, r - HALO, r + HALO))
    col = jnp.where(right == 0, j - HALO, TW + j)
    token = (row + TH) % TH * TW + (col + TW) % TW
    line = 3 * right + jnp.where(corner == 0, 0, 1 + r // HALO)
    lines = []
    for source in (from_left, from_right):
        found = source[flags_at(2 * SIDE), :]
        lines += [found[i : i + 1] for i in range(3)]
    return reach(row, col, flag_columns(line, token, lines))


def far_bias(far):
    key = iota((TOKENS, LANES), 0)
    token = far_token(key % ROWS, key // ROWS)
    flags = flag_columns(key * 0, token, [far[flags_at(ROWS, 1), :]])
    return jnp.where(flags > 0.5, 0.0, -jnp.inf)


def near_bias(bias, at, found):
    for r in range(HALO):
        bias[r, pl.ds(at, found.shape[0]), :] = jnp.where(found <= r + 1, 0.0, -jnp.inf)


def twice(x):
    first = iota(x.shape, 1) < HEAD
    return jnp.concatenate([jnp.where(first, x, 0.0), jnp.where(first, 0.0, x)], axis=0)


def own_columns(x):
    return jnp.concatenate([x[:HEAD, :TOKENS], x[HEAD:, TOKENS:]], axis=0)


def over_features(x):
    return jnp.concatenate(
        [
            jnp.broadcast_to(x[:, :TOKENS], (HEAD, TOKENS)),
            jnp.broadcast_to(x[:, TOKENS:], (HEAD, TOKENS)),
        ],
        axis=0,
    )


def scores(key, query):
    q1, q2, q3 = split3(twice(query * 0.125))
    k1, k2, k3 = split3(key)
    return across(
        jnp.concatenate([k1, k2, k1, k2, k3, k1], axis=1),
        jnp.concatenate([q1, q1, q2, q2, q1, q3], axis=1),
    )


def mixture(weight, value):
    p1, p2 = split2(weight)
    v1, v2 = split2(value.T)
    ones = jnp.ones((16, weight.shape[0]), jnp.bfloat16)
    zeros = jnp.zeros((16, weight.shape[0]), jnp.bfloat16)
    v1 = jnp.concatenate([v1, ones], axis=0)
    v2 = jnp.concatenate([v2, zeros], axis=0)
    mixed = jnp.dot(
        jnp.concatenate([v1, v1, v2], axis=1),
        jnp.concatenate([p1, p2, p1], axis=0),
        preferred_element_type=jnp.float32,
    )
    return own_columns(mixed[:LANES]), mixed[LANES : LANES + 1]


def first_kernel(
    offsets, radius, q, k, v, land, above, below, far0, far1, far2, far3, mixed, total, peak,
    near, beyond,
):
    fars = (far0, far1, far2, far3)
    near_bias(near, 0, own_reach(land))
    near_bias(near, TOKENS, edge_reach(above, below))
    for s, far in enumerate(fars):
        beyond[s] = far_bias(far)

    def gather(part, pair, at):
        pieces = [(k, v)[part][:, at]]
        pieces += [source[block(EDGE, pair, part), :] for source in (below, above)]
        pieces += [source[block(ROWS, pair, part), :] for source in fars]
        return jnp.concatenate(pieces, axis=0)

    def barrier(pair):
        bias = []
        for head in (2 * pair, 2 * pair + 1):
            rows = [near[radius[head] - 1]]
            for s in range(4):
                start = pl.multiple_of(offsets[s // 2, s % 2, head] * ROWS, ROWS)
                rows.append(beyond[s, pl.ds(start, ROWS), :])
            bias.append(jnp.concatenate(rows, axis=0))
        return jnp.concatenate(bias, axis=1)

    def body(pairs, ats):
        masked = [scores(gather(0, pair, at), q[:, at]) for pair, at in zip(pairs, ats)]
        masked = [x + barrier(pair) for x, pair in zip(masked, pairs)]
        tops = [jnp.max(x, axis=0, keepdims=True) for x in masked]
        weights = [jnp.exp(x - top) for x, top in zip(masked, tops)]
        mixes = [mixture(x, gather(1, *at)) for x, at in zip(weights, zip(pairs, ats))]
        for pair, at, top, (mix, weight) in zip(pairs, ats, tops, mixes):
            mixed[at, :] = mix
            total[pair] = jnp.broadcast_to(weight, (8, 2 * TOKENS))
            peak[pair] = jnp.broadcast_to(top, (8, 2 * TOKENS))

    body(range(PAIRS), [pl.ds(pair * LANES, LANES) for pair in range(PAIRS)])


def second_kernel(radius, q, from_left, from_right, mixed, total, peak, out, near):
    near_bias(near, 0, side_reach(from_left, from_right))

    def gather(part, pair):
        return jnp.concatenate(
            [source[block(2 * SIDE, pair, part), :] for source in (from_left, from_right)], axis=0
        )

    def barrier(pair):
        return jnp.concatenate([near[radius[head] - 1] for head in (2 * pair, 2 * pair + 1)], axis=1)

    def body(pairs, ats):
        masked = [scores(gather(0, pair), q[:, at]) for pair, at in zip(pairs, ats)]
        masked = [x + barrier(pair) for x, pair in zip(masked, pairs)]
        old = [peak[pair][0:1] for pair in pairs]
        tops = [jnp.maximum(jnp.max(x, axis=0, keepdims=True), y) for x, y in zip(masked, old)]
        weights = [jnp.exp(x - top) for x, top in zip(masked, tops)]
        mixes = [mixture(x, gather(1, pair)) for x, pair in zip(weights, pairs)]
        done = []
        for pair, at, top, before, (mix, weight) in zip(pairs, ats, tops, old, mixes):
            shrink = jnp.exp(before - top)
            inverse = 1.0 / (total[pair][0:1] * shrink + weight)
            done.append(
                mixed[at, :] * over_features(shrink * inverse) + mix * over_features(inverse)
            )
        for at, mix in zip(ats, done):
            out[:, at] = mix.T

    body(range(PAIRS), [pl.ds(pair * LANES, LANES) for pair in range(PAIRS)])


def shifted(value, axis, steps, periodic=True):
    count = lax.axis_size(axis)
    pairs = [
        (source, (source + steps) % count)
        for source in range(count)
        if periodic or 0 <= source + steps < count
    ]
    return lax.ppermute(value, axis, pairs)


def vmem(count):
    return [pl.BlockSpec(memory_space=pltpu.VMEM)] * count


def smem(count):
    return [pl.BlockSpec(memory_space=pltpu.SMEM)] * count


def payload(rows):
    return jax.ShapeDtypeStruct((2 * PAIRS * rows + FLAGS, LANES), jnp.float32)


def call(kernel, name, outs, smems, vmems, flops, moved, scratch=(), limit=16):
    return pl.pallas_call(
        kernel,
        out_shape=outs,
        in_specs=smem(smems) + vmem(vmems),
        out_specs=vmem(len(outs)),
        scratch_shapes=list(scratch),
        compiler_params=pltpu.CompilerParams(vmem_limit_bytes=limit << 20),
        cost_estimate=pl.CostEstimate(
            flops=flops, bytes_accessed=moved << 20, transcendentals=0
        ),
        name=name,
    )


def local(queries, key_vectors, value_vectors, land_mask, radius, offsets):
    q = queries.reshape(TOKENS, D)
    k = key_vectors.reshape(TOKENS, D)
    v = value_vectors.reshape(TOKENS, D)
    up, down = pl.pallas_call(
        edge_kernel,
        out_shape=[payload(EDGE)] * 2,
        in_specs=[pl.BlockSpec(memory_space=pltpu.HBM)] * 3,
        out_specs=vmem(2),
        scratch_shapes=[
            pltpu.VMEM((TH, TW), jnp.int32),
            pltpu.SemaphoreType.DMA((4 * PAIRS,)),
            pltpu.SemaphoreType.DMA,
        ],
        compiler_params=pltpu.CompilerParams(vmem_limit_bytes=58 << 20),
        cost_estimate=pl.CostEstimate(flops=1 << 16, bytes_accessed=2 << 20, transcendentals=0),
        name="edge",
    )(k, v, land_mask)
    k, v, land_mask, up, down = lax.optimization_barrier((k, v, land_mask, up, down))
    above = shifted(down, "lat", 1, False)
    below = shifted(up, "lat", -1, False)
    fars = call(far_kernel, "far", [payload(ROWS)] * 4, 1, 3, 1 << 20, 2)(
        offsets, k, v, land_mask
    )
    fars, arrived = list(fars), [None] * 4
    for s in (0, 2, 1, 3):
        level, heading = s // 2, s % 2
        distance = (1 - 2 * heading) * 2 ** (level + 1)
        if s == 3:
            arrived[2], fars[3] = lax.optimization_barrier((arrived[2], fars[3]))
        arrived[s] = shifted(fars[s], "lon", -distance)
    to_right, to_left = call(
        side_kernel, "side", [payload(2 * SIDE)] * 2, 0, 5, 1 << 33, 3
    )(k, v, land_mask, above, below)
    from_left = shifted(to_right, "lon", 1)
    from_right = shifted(to_left, "lon", -1)
    line = jax.ShapeDtypeStruct((PAIRS, 8, 2 * TOKENS), jnp.float32)
    partial = call(
        first_kernel, "first", [jax.ShapeDtypeStruct((D, TOKENS), jnp.float32), line, line],
        2, 10, 1 << 34, 6,
        [
            pltpu.VMEM((HALO, 2 * TOKENS, LANES), jnp.float32),
            pltpu.VMEM((4, TOKENS, LANES), jnp.float32),
        ],
        24,
    )(offsets, radius, q, k, v, land_mask, above, below, *arrived)
    [result] = call(
        second_kernel, "second", [jax.ShapeDtypeStruct((TOKENS, D), jnp.float32)],
        1, 6, 1 << 28, 4, [pltpu.VMEM((HALO, TOKENS, LANES), jnp.float32)],
    )(radius, q, from_left, from_right, *partial)
    return result.reshape(TH, TW, D)


def solution(mesh):
    tile = P("lat", "lon", None)
    in_specs = (tile, tile, tile, P("lat", "lon"), P(), P())
    return jax.shard_map(local, mesh=mesh, in_specs=in_specs, out_specs=tile, check_vma=False)
```

```python
import functools

import jax
import jax.numpy as jnp
from jax import lax
from jax.experimental import pallas as pl
from jax.experimental.pallas import tpu as pltpu
from jax.sharding import PartitionSpec as P

TH = 8
TW = 16
TOKENS = TH * TW
HALO = 4
RATE = 4
LEVELS = 2
HEADS = 16
D = 1024
HEAD = D // HEADS
LANES = 128
PAIRS = D // LANES
ROWS = TOKENS // RATE
SIDE = TH * HALO
EDGE = TW * HALO
FLAGS = 8


def iota(shape, dim):
    return lax.broadcasted_iota(jnp.int32, shape, dim)


def land_line(land):
    spread = (iota((TW, TOKENS), 1) % TW == iota((TW, TOKENS), 0)).astype(jnp.float32)
    wide = jnp.dot(land.astype(jnp.float32), spread, preferred_element_type=jnp.float32)
    own = iota((TH, TOKENS), 1) // TW == iota((TH, TOKENS), 0)
    line = jnp.sum(jnp.where(own, wide, 0.0), axis=0, keepdims=True)
    return jnp.broadcast_to(line, (TH, TOKENS))


def block(rows, pair, part):
    return pl.ds((2 * pair + part) * rows, rows)


def flags_at(rows, count=FLAGS):
    return pl.ds(2 * PAIRS * rows, count)


def side_rows(read, to_right, count):
    low = iota((8, LANES), 0) < HALO
    found = []
    for r in range(0, count, 2):
        at = r * TW + (TW - TH if to_right else 0)
        even, odd = read(at), read(at + TW)
        if to_right:
            found.append(jnp.where(low, pltpu.roll(even, HALO, 0), odd))
        else:
            found.append(jnp.where(low, even, pltpu.roll(odd, HALO, 0)))
    return found


def dilated_rows(source, at):
    quarter = iota((8, LANES), 0) % RATE
    found = [[] for _ in range(RATE)]
    for g in range(ROWS // 8):
        tiles = [source[pl.ds((g * RATE + i) * 8, 8), at] for i in range(RATE)]
        turned = [[t] + [pltpu.roll(t, d, 0) for d in range(1, RATE)] for t in tiles]
        for o in range(RATE):
            rows = turned[0][-o % RATE]
            for i in range(1, RATE):
                rows = jnp.where(quarter == i, turned[i][(i - o) % RATE], rows)
            found[o].append(rows)
    return [jnp.concatenate(rows, axis=0) for rows in found]


def far_token(n, o):
    i = n % RATE
    half = (n % 8) // RATE
    half = jnp.where(i < o, 1 - half, half)
    return (n // 8 * RATE + i) * 8 + o + RATE * half


def edge_kernel(k, v, land, up, down, flags, sems, flags_sem):
    fetch = pltpu.make_async_copy(land, flags, flags_sem)
    fetch.start()
    copies = []
    for pair in range(PAIRS):
        for part, source in enumerate((k, v)):
            for which, (target, start) in enumerate(((up, 0), (down, TOKENS - EDGE))):
                copies.append(
                    pltpu.make_async_copy(
                        source.at[pl.ds(start, EDGE), pl.ds(pair * LANES, LANES)],
                        target.at[block(EDGE, pair, part), :],
                        sems.at[(2 * pair + part) * 2 + which],
                    )
                )
                copies[-1].start()
    fetch.wait()
    line = land_line(flags[...])
    up[flags_at(EDGE), :] = line
    down[flags_at(EDGE), :] = line
    for copy in copies:
        copy.wait()


def far_kernel(offsets, k, v, land, far0, far1, far2, far3):
    line = land_line(land[...])
    first = iota((ROWS, LANES), 1) < HEAD
    fars = (far0, far1, far2, far3)
    for far in fars:
        far[flags_at(ROWS), :] = line
    for pair in range(PAIRS):
        at = pl.ds(pair * LANES, LANES)
        for part, source in enumerate((k, v)):
            rows = dilated_rows(source, at)
            for s, far in enumerate(fars):
                want = jnp.where(
                    first,
                    offsets[s // 2, s % 2, 2 * pair],
                    offsets[s // 2, s % 2, 2 * pair + 1],
                )
                picked = rows[0]
                for o in range(1, RATE):
                    picked = jnp.where(want == o, rows[o], picked)
                far[block(ROWS, pair, part), :] = picked


def side_kernel(k, v, land, above, below, to_right, to_left):
    for pair in range(PAIRS):
        at = pl.ds(pair * LANES, LANES)
        for part, own in enumerate((k, v)):
            start = (2 * pair + part) * EDGE
            for target, right in ((to_right, True), (to_left, False)):
                rows = side_rows(lambda row: own[pl.ds(row, 8), at], right, TH)
                for source in (above, below):
                    rows += side_rows(lambda row: source[pl.ds(start + row, 8), :], right, HALO)
                target[block(2 * SIDE, pair, part), :] = jnp.concatenate(rows, axis=0)
    row = iota((FLAGS, LANES), 0)
    near = land_line(land[...])
    line = jnp.where(
        row == 0, near, jnp.where(row == 1, above[flags_at(EDGE), :], below[flags_at(EDGE), :])
    )
    to_right[flags_at(2 * SIDE), :] = line
    to_left[flags_at(2 * SIDE), :] = line


def split2(x):
    high = x.astype(jnp.bfloat16)
    low = (x - high.astype(jnp.float32)).astype(jnp.bfloat16)
    return high, low


def split3(x):
    high = x.astype(jnp.bfloat16)
    rest = x - high.astype(jnp.float32)
    mid = rest.astype(jnp.bfloat16)
    low = (rest - mid.astype(jnp.float32)).astype(jnp.bfloat16)
    return high, mid, low


def spacing(row, col):
    query = iota(row.shape, 1)
    return jnp.maximum(jnp.abs(query // TW - row), jnp.abs(query % TW - col))


def across(x, y):
    return lax.dot_general(x, y, (((1,), (1,)), ((), ())), preferred_element_type=jnp.float32)


def flag_columns(line, token, lines):
    shape = (line.shape[0], LANES)
    spot = line * LANES + token - iota(shape, 1)
    pick = [(spot == at * LANES).astype(jnp.bfloat16) for at in range(len(lines))]
    rows = [jnp.broadcast_to(row, (LANES, LANES)).astype(jnp.bfloat16) for row in lines]
    return across(jnp.concatenate(pick, axis=1), jnp.concatenate(rows, axis=1))


def reach(row, col, flags):
    gap = spacing(row, col)
    return jnp.where((flags > 0.5) | (gap == 0), gap, 99)


def own_reach(land):
    key = iota((TOKENS, LANES), 0)
    return reach(key // TW, key % TW, flag_columns(key * 0, key, [land_line(land[...])[0:1]]))


def edge_reach(above, below):
    key = iota((2 * EDGE, LANES), 0)
    row = jnp.where(key < EDGE, TH + key // TW, key // TW - TH)
    lines = [source[flags_at(EDGE, 1), :] for source in (below, above)]
    return reach(row, key % TW, flag_columns(key // EDGE, key, lines))


def side_reach(from_left, from_right):
    key = iota((4 * SIDE, LANES), 0)
    right, corner = key // (2 * SIDE), key // SIDE % 2
    r, j = key % SIDE // HALO, key % HALO
    row = jnp.where(corner == 0, r, jnp.where(r < HALO, r - HALO, r + HALO))
    col = jnp.where(right == 0, j - HALO, TW + j)
    token = (row + TH) % TH * TW + (col + TW) % TW
    line = 3 * right + jnp.where(corner == 0, 0, 1 + r // HALO)
    lines = []
    for source in (from_left, from_right):
        found = source[flags_at(2 * SIDE), :]
        lines += [found[i : i + 1] for i in range(3)]
    return reach(row, col, flag_columns(line, token, lines))


def far_bias(far):
    key = iota((TOKENS, LANES), 0)
    token = far_token(key % ROWS, key // ROWS)
    flags = flag_columns(key * 0, token, [far[flags_at(ROWS, 1), :]])
    return jnp.where(flags > 0.5, 0.0, -jnp.inf)


def near_bias(bias, at, found):
    for r in range(HALO):
        bias[r, pl.ds(at, found.shape[0]), :] = jnp.where(found <= r + 1, 0.0, -jnp.inf)


def twice(x):
    first = iota(x.shape, 1) < HEAD
    return jnp.concatenate([jnp.where(first, x, 0.0), jnp.where(first, 0.0, x)], axis=0)


def own_columns(x):
    return jnp.concatenate([x[:HEAD, :TOKENS], x[HEAD:, TOKENS:]], axis=0)


def over_features(x):
    return jnp.concatenate(
        [
            jnp.broadcast_to(x[:, :TOKENS], (HEAD, TOKENS)),
            jnp.broadcast_to(x[:, TOKENS:], (HEAD, TOKENS)),
        ],
        axis=0,
    )


def scores(key, query):
    q1, q2, q3 = split3(twice(query * 0.125))
    k1, k2, k3 = split3(key)
    return across(
        jnp.concatenate([k1, k2, k1, k2, k3, k1], axis=1),
        jnp.concatenate([q1, q1, q2, q2, q1, q3], axis=1),
    )


def mixture(weight, value):
    p1, p2 = split2(weight)
    v1, v2 = split2(value.T)
    ones = jnp.ones((16, weight.shape[0]), jnp.bfloat16)
    zeros = jnp.zeros((16, weight.shape[0]), jnp.bfloat16)
    v1 = jnp.concatenate([v1, ones], axis=0)
    v2 = jnp.concatenate([v2, zeros], axis=0)
    mixed = jnp.dot(
        jnp.concatenate([v1, v1, v2], axis=1),
        jnp.concatenate([p1, p2, p1], axis=0),
        preferred_element_type=jnp.float32,
    )
    return own_columns(mixed[:LANES]), mixed[LANES : LANES + 1]


def first_kernel(
    offsets, radius, q, k, v, land, above, below, far0, far1, far2, far3, mixed, total, peak,
    near, beyond,
):
    fars = (far0, far1, far2, far3)
    near_bias(near, 0, own_reach(land))
    near_bias(near, TOKENS, edge_reach(above, below))
    for s, far in enumerate(fars):
        beyond[s] = far_bias(far)

    def gather(part, pair, at):
        pieces = [(k, v)[part][:, at]]
        pieces += [source[block(EDGE, pair, part), :] for source in (below, above)]
        pieces += [source[block(ROWS, pair, part), :] for source in fars]
        return jnp.concatenate(pieces, axis=0)

    def barrier(pair):
        bias = []
        for head in (2 * pair, 2 * pair + 1):
            rows = [near[radius[head] - 1]]
            for s in range(4):
                start = pl.multiple_of(offsets[s // 2, s % 2, head] * ROWS, ROWS)
                rows.append(beyond[s, pl.ds(start, ROWS), :])
            bias.append(jnp.concatenate(rows, axis=0))
        return jnp.concatenate(bias, axis=1)

    def body(pairs, ats):
        masked = [scores(gather(0, pair, at), q[:, at]) for pair, at in zip(pairs, ats)]
        masked = [x + barrier(pair) for x, pair in zip(masked, pairs)]
        tops = [jnp.max(x, axis=0, keepdims=True) for x in masked]
        weights = [jnp.exp(x - top) for x, top in zip(masked, tops)]
        mixes = [mixture(x, gather(1, *at)) for x, at in zip(weights, zip(pairs, ats))]
        for pair, at, top, (mix, weight) in zip(pairs, ats, tops, mixes):
            mixed[at, :] = mix
            total[pair] = jnp.broadcast_to(weight, (8, 2 * TOKENS))
            peak[pair] = jnp.broadcast_to(top, (8, 2 * TOKENS))

    body(range(PAIRS), [pl.ds(pair * LANES, LANES) for pair in range(PAIRS)])


def second_kernel(radius, q, from_left, from_right, mixed, total, peak, out, near):
    near_bias(near, 0, side_reach(from_left, from_right))

    def gather(part, pair):
        return jnp.concatenate(
            [source[block(2 * SIDE, pair, part), :] for source in (from_left, from_right)], axis=0
        )

    def barrier(pair):
        return jnp.concatenate([near[radius[head] - 1] for head in (2 * pair, 2 * pair + 1)], axis=1)

    def body(pairs, ats):
        masked = [scores(gather(0, pair), q[:, at]) for pair, at in zip(pairs, ats)]
        masked = [x + barrier(pair) for x, pair in zip(masked, pairs)]
        old = [peak[pair][0:1] for pair in pairs]
        tops = [jnp.maximum(jnp.max(x, axis=0, keepdims=True), y) for x, y in zip(masked, old)]
        weights = [jnp.exp(x - top) for x, top in zip(masked, tops)]
        mixes = [mixture(x, gather(1, pair)) for x, pair in zip(weights, pairs)]
        done = []
        for pair, at, top, before, (mix, weight) in zip(pairs, ats, tops, old, mixes):
            shrink = jnp.exp(before - top)
            inverse = 1.0 / (total[pair][0:1] * shrink + weight)
            done.append(
                mixed[at, :] * over_features(shrink * inverse) + mix * over_features(inverse)
            )
        for at, mix in zip(ats, done):
            out[:, at] = mix.T

    body(range(PAIRS), [pl.ds(pair * LANES, LANES) for pair in range(PAIRS)])


def shifted(value, axis, steps, periodic=True):
    count = lax.axis_size(axis)
    pairs = [
        (source, (source + steps) % count)
        for source in range(count)
        if periodic or 0 <= source + steps < count
    ]
    return lax.ppermute(value, axis, pairs)


def vmem(count):
    return [pl.BlockSpec(memory_space=pltpu.VMEM)] * count


def smem(count):
    return [pl.BlockSpec(memory_space=pltpu.SMEM)] * count


def payload(rows):
    return jax.ShapeDtypeStruct((2 * PAIRS * rows + FLAGS, LANES), jnp.float32)


def call(kernel, name, outs, smems, vmems, flops, moved, scratch=(), limit=16):
    return pl.pallas_call(
        kernel,
        out_shape=outs,
        in_specs=smem(smems) + vmem(vmems),
        out_specs=vmem(len(outs)),
        scratch_shapes=list(scratch),
        compiler_params=pltpu.CompilerParams(vmem_limit_bytes=limit << 20),
        cost_estimate=pl.CostEstimate(
            flops=flops, bytes_accessed=moved << 20, transcendentals=0
        ),
        name=name,
    )


def local(queries, key_vectors, value_vectors, land_mask, radius, offsets):
    q = queries.reshape(TOKENS, D)
    k = key_vectors.reshape(TOKENS, D)
    v = value_vectors.reshape(TOKENS, D)
    up, down = pl.pallas_call(
        edge_kernel,
        out_shape=[payload(EDGE)] * 2,
        in_specs=[pl.BlockSpec(memory_space=pltpu.HBM)] * 3,
        out_specs=vmem(2),
        scratch_shapes=[
            pltpu.VMEM((TH, TW), jnp.int32),
            pltpu.SemaphoreType.DMA((4 * PAIRS,)),
            pltpu.SemaphoreType.DMA,
        ],
        compiler_params=pltpu.CompilerParams(vmem_limit_bytes=16 << 20),
        cost_estimate=pl.CostEstimate(flops=1 << 16, bytes_accessed=2 << 20, transcendentals=0),
        name="edge",
    )(*(pltpu.with_memory_space_constraint(x, pltpu.HBM) for x in (k, v, land_mask)))
    k, v, land_mask, up, down = lax.optimization_barrier((k, v, land_mask, up, down))
    above = shifted(down, "lat", 1, False)
    below = shifted(up, "lat", -1, False)
    fars = call(far_kernel, "far", [payload(ROWS)] * 4, 1, 3, 1 << 20, 2)(
        offsets, k, v, land_mask
    )
    fars, arrived = list(fars), [None] * 4
    for s in (0, 2, 1, 3):
        level, heading = s // 2, s % 2
        distance = (1 - 2 * heading) * 2 ** (level + 1)
        if s == 3:
            arrived[2], fars[3] = lax.optimization_barrier((arrived[2], fars[3]))
        arrived[s] = shifted(fars[s], "lon", -distance)
    to_right, to_left = call(
        side_kernel, "side", [payload(2 * SIDE)] * 2, 0, 5, 1 << 33, 3
    )(k, v, land_mask, above, below)
    from_left = shifted(to_right, "lon", 1)
    from_right = shifted(to_left, "lon", -1)
    line = jax.ShapeDtypeStruct((PAIRS, 8, 2 * TOKENS), jnp.float32)
    partial = call(
        first_kernel, "first", [jax.ShapeDtypeStruct((D, TOKENS), jnp.float32), line, line],
        2, 10, 1 << 34, 6,
        [
            pltpu.VMEM((HALO, 2 * TOKENS, LANES), jnp.float32),
            pltpu.VMEM((4, TOKENS, LANES), jnp.float32),
        ],
        24,
    )(offsets, radius, q, k, v, land_mask, above, below, *arrived)
    [result] = call(
        second_kernel, "second", [jax.ShapeDtypeStruct((TOKENS, D), jnp.float32)],
        1, 6, 1 << 28, 4, [pltpu.VMEM((HALO, TOKENS, LANES), jnp.float32)],
    )(radius, q, from_left, from_right, *partial)
    return result.reshape(TH, TW, D)


def solution(mesh):
    tile = P("lat", "lon", None)
    in_specs = (tile, tile, tile, P("lat", "lon"), P(), P())
    return jax.shard_map(local, mesh=mesh, in_specs=in_specs, out_specs=tile, check_vma=False)
```

```python
import functools

import jax
import jax.numpy as jnp
from jax import lax
from jax.experimental import pallas as pl
from jax.experimental.pallas import tpu as pltpu
from jax.sharding import PartitionSpec as P

TH = 8
TW = 16
TOKENS = TH * TW
HALO = 4
RATE = 4
LEVELS = 2
HEADS = 16
D = 1024
HEAD = D // HEADS
LANES = 128
PAIRS = D // LANES
ROWS = TOKENS // RATE
SIDE = TH * HALO
EDGE = TW * HALO
FLAGS = 8


def iota(shape, dim):
    return lax.broadcasted_iota(jnp.int32, shape, dim)


def land_line(land):
    spread = (iota((TW, TOKENS), 1) % TW == iota((TW, TOKENS), 0)).astype(jnp.float32)
    wide = jnp.dot(land.astype(jnp.float32), spread, preferred_element_type=jnp.float32)
    own = iota((TH, TOKENS), 1) // TW == iota((TH, TOKENS), 0)
    line = jnp.sum(jnp.where(own, wide, 0.0), axis=0, keepdims=True)
    return jnp.broadcast_to(line, (TH, TOKENS))


def block(rows, pair, part):
    return pl.ds((2 * pair + part) * rows, rows)


def flags_at(rows, count=FLAGS):
    return pl.ds(2 * PAIRS * rows, count)


def side_rows(read, to_right, count):
    low = iota((8, LANES), 0) < HALO
    found = []
    for r in range(0, count, 2):
        at = r * TW + (TW - TH if to_right else 0)
        even, odd = read(at), read(at + TW)
        if to_right:
            found.append(jnp.where(low, pltpu.roll(even, HALO, 0), odd))
        else:
            found.append(jnp.where(low, even, pltpu.roll(odd, HALO, 0)))
    return found


def dilated_rows(source, at):
    quarter = iota((8, LANES), 0) % RATE
    found = [[] for _ in range(RATE)]
    for g in range(ROWS // 8):
        tiles = [source[pl.ds((g * RATE + i) * 8, 8), at] for i in range(RATE)]
        turned = [[t] + [pltpu.roll(t, d, 0) for d in range(1, RATE)] for t in tiles]
        for o in range(RATE):
            rows = turned[0][-o % RATE]
            for i in range(1, RATE):
                rows = jnp.where(quarter == i, turned[i][(i - o) % RATE], rows)
            found[o].append(rows)
    return [jnp.concatenate(rows, axis=0) for rows in found]


def far_token(n, o):
    i = n % RATE
    half = (n % 8) // RATE
    half = jnp.where(i < o, 1 - half, half)
    return (n // 8 * RATE + i) * 8 + o + RATE * half


def edge_kernel(k, v, land, up, down, flags, sems, flags_sem):
    fetch = pltpu.make_async_copy(land, flags, flags_sem)
    fetch.start()
    copies = []
    for pair in range(PAIRS):
        for part, source in enumerate((k, v)):
            for which, (target, start) in enumerate(((up, 0), (down, TOKENS - EDGE))):
                copies.append(
                    pltpu.make_async_copy(
                        source.at[pl.ds(start, EDGE), pl.ds(pair * LANES, LANES)],
                        target.at[block(EDGE, pair, part), :],
                        sems.at[(2 * pair + part) * 2 + which],
                    )
                )
                copies[-1].start()
    fetch.wait()
    line = land_line(flags[...])
    up[flags_at(EDGE), :] = line
    down[flags_at(EDGE), :] = line
    for copy in copies:
        copy.wait()


def far_kernel(offsets, k, v, land, far0, far1, far2, far3):
    line = land_line(land[...])
    first = iota((ROWS, LANES), 1) < HEAD
    fars = (far0, far1, far2, far3)
    for far in fars:
        far[flags_at(ROWS), :] = line
    for pair in range(PAIRS):
        at = pl.ds(pair * LANES, LANES)
        for part, source in enumerate((k, v)):
            rows = dilated_rows(source, at)
            for s, far in enumerate(fars):
                want = jnp.where(
                    first,
                    offsets[s // 2, s % 2, 2 * pair],
                    offsets[s // 2, s % 2, 2 * pair + 1],
                )
                picked = rows[0]
                for o in range(1, RATE):
                    picked = jnp.where(want == o, rows[o], picked)
                far[block(ROWS, pair, part), :] = picked


def on_odd():
    return lax.axis_index("lon") % 2 == 1


def side_kernel(k, v, land, above, below, to_cross, to_near):
    odd = on_odd()
    for pair in range(PAIRS):
        at = pl.ds(pair * LANES, LANES)
        for part, own in enumerate((k, v)):
            start = (2 * pair + part) * EDGE
            both = []
            for right in (True, False):
                rows = side_rows(lambda row: own[pl.ds(row, 8), at], right, TH)
                for source in (above, below):
                    rows += side_rows(lambda row: source[pl.ds(start + row, 8), :], right, HALO)
                both.append(jnp.concatenate(rows, axis=0))
            to_cross[block(2 * SIDE, pair, part), :] = jnp.where(odd, both[0], both[1])
            to_near[block(2 * SIDE, pair, part), :] = jnp.where(odd, both[1], both[0])
    row = iota((FLAGS, LANES), 0)
    near = land_line(land[...])
    line = jnp.where(
        row == 0, near, jnp.where(row == 1, above[flags_at(EDGE), :], below[flags_at(EDGE), :])
    )
    to_cross[flags_at(2 * SIDE), :] = line
    to_near[flags_at(2 * SIDE), :] = line


def split2(x):
    high = x.astype(jnp.bfloat16)
    low = (x - high.astype(jnp.float32)).astype(jnp.bfloat16)
    return high, low


def split3(x):
    high = x.astype(jnp.bfloat16)
    rest = x - high.astype(jnp.float32)
    mid = rest.astype(jnp.bfloat16)
    low = (rest - mid.astype(jnp.float32)).astype(jnp.bfloat16)
    return high, mid, low


def spacing(row, col):
    query = iota(row.shape, 1)
    return jnp.maximum(jnp.abs(query // TW - row), jnp.abs(query % TW - col))


def across(x, y):
    return lax.dot_general(x, y, (((1,), (1,)), ((), ())), preferred_element_type=jnp.float32)


def flag_columns(line, token, lines):
    shape = (line.shape[0], LANES)
    spot = line * LANES + token - iota(shape, 1)
    pick = [(spot == at * LANES).astype(jnp.bfloat16) for at in range(len(lines))]
    rows = [jnp.broadcast_to(row, (LANES, LANES)).astype(jnp.bfloat16) for row in lines]
    return across(jnp.concatenate(pick, axis=1), jnp.concatenate(rows, axis=1))


def reach(row, col, flags):
    gap = spacing(row, col)
    return jnp.where((flags > 0.5) | (gap == 0), gap, 99)


def own_reach(land):
    key = iota((TOKENS, LANES), 0)
    return reach(key // TW, key % TW, flag_columns(key * 0, key, [land_line(land[...])[0:1]]))


def edge_reach(above, below):
    key = iota((2 * EDGE, LANES), 0)
    row = jnp.where(key < EDGE, TH + key // TW, key // TW - TH)
    lines = [source[flags_at(EDGE, 1), :] for source in (below, above)]
    return reach(row, key % TW, flag_columns(key // EDGE, key, lines))


def side_reach(crossed, nearby):
    key = iota((4 * SIDE, LANES), 0)
    which, corner = key // (2 * SIDE), key // SIDE % 2
    right = jnp.where(on_odd(), 1 - which, which)
    r, j = key % SIDE // HALO, key % HALO
    row = jnp.where(corner == 0, r, jnp.where(r < HALO, r - HALO, r + HALO))
    col = jnp.where(right == 0, j - HALO, TW + j)
    token = (row + TH) % TH * TW + (col + TW) % TW
    line = 3 * which + jnp.where(corner == 0, 0, 1 + r // HALO)
    lines = []
    for source in (crossed, nearby):
        found = source[flags_at(2 * SIDE), :]
        lines += [found[i : i + 1] for i in range(3)]
    return reach(row, col, flag_columns(line, token, lines))


def far_bias(far):
    key = iota((TOKENS, LANES), 0)
    token = far_token(key % ROWS, key // ROWS)
    flags = flag_columns(key * 0, token, [far[flags_at(ROWS, 1), :]])
    return jnp.where(flags > 0.5, 0.0, -jnp.inf)


def near_bias(bias, at, found):
    for r in range(HALO):
        bias[r, pl.ds(at, found.shape[0]), :] = jnp.where(found <= r + 1, 0.0, -jnp.inf)


def twice(x):
    first = iota(x.shape, 1) < HEAD
    return jnp.concatenate([jnp.where(first, x, 0.0), jnp.where(first, 0.0, x)], axis=0)


def own_columns(x):
    return jnp.concatenate([x[:HEAD, :TOKENS], x[HEAD:, TOKENS:]], axis=0)


def over_features(x):
    return jnp.concatenate(
        [
            jnp.broadcast_to(x[:, :TOKENS], (HEAD, TOKENS)),
            jnp.broadcast_to(x[:, TOKENS:], (HEAD, TOKENS)),
        ],
        axis=0,
    )


def scores(key, query):
    q1, q2, q3 = split3(twice(query * 0.125))
    k1, k2, k3 = split3(key)
    return across(
        jnp.concatenate([k1, k2, k1, k2, k3, k1], axis=1),
        jnp.concatenate([q1, q1, q2, q2, q1, q3], axis=1),
    )


def mixture(weight, value):
    p1, p2 = split2(weight)
    v1, v2 = split2(value.T)
    ones = jnp.ones((16, weight.shape[0]), jnp.bfloat16)
    zeros = jnp.zeros((16, weight.shape[0]), jnp.bfloat16)
    v1 = jnp.concatenate([v1, ones], axis=0)
    v2 = jnp.concatenate([v2, zeros], axis=0)
    mixed = jnp.dot(
        jnp.concatenate([v1, v1, v2], axis=1),
        jnp.concatenate([p1, p2, p1], axis=0),
        preferred_element_type=jnp.float32,
    )
    return own_columns(mixed[:LANES]), mixed[LANES : LANES + 1]


def first_kernel(
    offsets, radius, q, k, v, land, above, below, far0, far1, far2, far3, mixed, total, peak,
    near, beyond,
):
    fars = (far0, far1, far2, far3)
    near_bias(near, 0, own_reach(land))
    near_bias(near, TOKENS, edge_reach(above, below))
    for s, far in enumerate(fars):
        beyond[s] = far_bias(far)

    def gather(part, pair, at):
        pieces = [(k, v)[part][:, at]]
        pieces += [source[block(EDGE, pair, part), :] for source in (below, above)]
        pieces += [source[block(ROWS, pair, part), :] for source in fars]
        return jnp.concatenate(pieces, axis=0)

    def barrier(pair):
        bias = []
        for head in (2 * pair, 2 * pair + 1):
            rows = [near[radius[head] - 1]]
            for s in range(4):
                start = pl.multiple_of(offsets[s // 2, s % 2, head] * ROWS, ROWS)
                rows.append(beyond[s, pl.ds(start, ROWS), :])
            bias.append(jnp.concatenate(rows, axis=0))
        return jnp.concatenate(bias, axis=1)

    def body(pairs, ats):
        masked = [scores(gather(0, pair, at), q[:, at]) for pair, at in zip(pairs, ats)]
        masked = [x + barrier(pair) for x, pair in zip(masked, pairs)]
        tops = [jnp.max(x, axis=0, keepdims=True) for x in masked]
        weights = [jnp.exp(x - top) for x, top in zip(masked, tops)]
        mixes = [mixture(x, gather(1, *at)) for x, at in zip(weights, zip(pairs, ats))]
        for pair, at, top, (mix, weight) in zip(pairs, ats, tops, mixes):
            mixed[at, :] = mix
            total[pair] = jnp.broadcast_to(weight, (8, 2 * TOKENS))
            peak[pair] = jnp.broadcast_to(top, (8, 2 * TOKENS))

    body(range(PAIRS), [pl.ds(pair * LANES, LANES) for pair in range(PAIRS)])


def second_kernel(radius, q, crossed, nearby, mixed, total, peak, out, near):
    near_bias(near, 0, side_reach(crossed, nearby))

    def gather(part, pair):
        return jnp.concatenate(
            [source[block(2 * SIDE, pair, part), :] for source in (crossed, nearby)], axis=0
        )

    def barrier(pair):
        return jnp.concatenate([near[radius[head] - 1] for head in (2 * pair, 2 * pair + 1)], axis=1)

    def body(pairs, ats):
        masked = [scores(gather(0, pair), q[:, at]) for pair, at in zip(pairs, ats)]
        masked = [x + barrier(pair) for x, pair in zip(masked, pairs)]
        old = [peak[pair][0:1] for pair in pairs]
        tops = [jnp.maximum(jnp.max(x, axis=0, keepdims=True), y) for x, y in zip(masked, old)]
        weights = [jnp.exp(x - top) for x, top in zip(masked, tops)]
        mixes = [mixture(x, gather(1, pair)) for x, pair in zip(weights, pairs)]
        done = []
        for pair, at, top, before, (mix, weight) in zip(pairs, ats, tops, old, mixes):
            shrink = jnp.exp(before - top)
            inverse = 1.0 / (total[pair][0:1] * shrink + weight)
            done.append(
                mixed[at, :] * over_features(shrink * inverse) + mix * over_features(inverse)
            )
        for at, mix in zip(ats, done):
            out[:, at] = mix.T

    body(range(PAIRS), [pl.ds(pair * LANES, LANES) for pair in range(PAIRS)])


def shifted(value, axis, steps, periodic=True):
    count = lax.axis_size(axis)
    pairs = [
        (source, (source + steps) % count)
        for source in range(count)
        if periodic or 0 <= source + steps < count
    ]
    return lax.ppermute(value, axis, pairs)


def swapped(value, axis, first):
    count = lax.axis_size(axis)
    pairs = [
        (source, (source + (1 if source % 2 == first else -1)) % count) for source in range(count)
    ]
    return lax.ppermute(value, axis, pairs)


def vmem(count):
    return [pl.BlockSpec(memory_space=pltpu.VMEM)] * count


def smem(count):
    return [pl.BlockSpec(memory_space=pltpu.SMEM)] * count


def payload(rows):
    return jax.ShapeDtypeStruct((2 * PAIRS * rows + FLAGS, LANES), jnp.float32)


def call(kernel, name, outs, smems, vmems, flops, moved, scratch=(), limit=16):
    return pl.pallas_call(
        kernel,
        out_shape=outs,
        in_specs=smem(smems) + vmem(vmems),
        out_specs=vmem(len(outs)),
        scratch_shapes=list(scratch),
        compiler_params=pltpu.CompilerParams(vmem_limit_bytes=limit << 20),
        cost_estimate=pl.CostEstimate(
            flops=flops, bytes_accessed=moved << 20, transcendentals=0
        ),
        name=name,
    )


def local(queries, key_vectors, value_vectors, land_mask, radius, offsets):
    q = queries.reshape(TOKENS, D)
    k = key_vectors.reshape(TOKENS, D)
    v = value_vectors.reshape(TOKENS, D)
    up, down = pl.pallas_call(
        edge_kernel,
        out_shape=[payload(EDGE)] * 2,
        in_specs=[pl.BlockSpec(memory_space=pltpu.HBM)] * 3,
        out_specs=vmem(2),
        scratch_shapes=[
            pltpu.VMEM((TH, TW), jnp.int32),
            pltpu.SemaphoreType.DMA((4 * PAIRS,)),
            pltpu.SemaphoreType.DMA,
        ],
        compiler_params=pltpu.CompilerParams(vmem_limit_bytes=16 << 20),
        cost_estimate=pl.CostEstimate(flops=1 << 16, bytes_accessed=2 << 20, transcendentals=0),
        name="edge",
    )(*(pltpu.with_memory_space_constraint(x, pltpu.HBM) for x in (k, v, land_mask)))
    k, v, land_mask, up, down = lax.optimization_barrier((k, v, land_mask, up, down))
    above = shifted(down, "lat", 1, False)
    below = shifted(up, "lat", -1, False)
    fars = call(far_kernel, "far", [payload(ROWS)] * 4, 1, 3, 1 << 20, 2)(
        offsets, k, v, land_mask
    )
    fars, arrived = list(fars), [None] * 4
    for s in (0, 2, 1, 3):
        level, heading = s // 2, s % 2
        distance = (1 - 2 * heading) * 2 ** (level + 1)
        if s == 3:
            arrived[2], fars[3] = lax.optimization_barrier((arrived[2], fars[3]))
        arrived[s] = shifted(fars[s], "lon", -distance)
    to_cross, to_near = call(
        side_kernel, "side", [payload(2 * SIDE)] * 2, 0, 5, 1 << 33, 3
    )(k, v, land_mask, above, below)
    crossed = swapped(to_cross, "lon", 1)
    nearby = swapped(to_near, "lon", 0)
    line = jax.ShapeDtypeStruct((PAIRS, 8, 2 * TOKENS), jnp.float32)
    partial = call(
        first_kernel, "first", [jax.ShapeDtypeStruct((D, TOKENS), jnp.float32), line, line],
        2, 10, 1 << 34, 6,
        [
            pltpu.VMEM((HALO, 2 * TOKENS, LANES), jnp.float32),
            pltpu.VMEM((4, TOKENS, LANES), jnp.float32),
        ],
        24,
    )(offsets, radius, q, k, v, land_mask, above, below, *arrived)
    [result] = call(
        second_kernel, "second", [jax.ShapeDtypeStruct((TOKENS, D), jnp.float32)],
        1, 6, 1 << 28, 4, [pltpu.VMEM((HALO, TOKENS, LANES), jnp.float32)],
    )(radius, q, crossed, nearby, *partial)
    return result.reshape(TH, TW, D)


def solution(mesh):
    tile = P("lat", "lon", None)
    in_specs = (tile, tile, tile, P("lat", "lon"), P(), P())
    return jax.shard_map(local, mesh=mesh, in_specs=in_specs, out_specs=tile, check_vma=False)
```

```python
import functools

import jax
import jax.numpy as jnp
from jax import lax
from jax.experimental import pallas as pl
from jax.experimental.pallas import tpu as pltpu
from jax.sharding import PartitionSpec as P

TH = 8
TW = 16
TOKENS = TH * TW
HALO = 4
RATE = 4
LEVELS = 2
HEADS = 16
D = 1024
HEAD = D // HEADS
LANES = 128
PAIRS = D // LANES
ROWS = TOKENS // RATE
SIDE = TH * HALO
EDGE = TW * HALO
FLAGS = 8


def iota(shape, dim):
    return lax.broadcasted_iota(jnp.int32, shape, dim)


def land_line(land):
    spread = (iota((TW, TOKENS), 1) % TW == iota((TW, TOKENS), 0)).astype(jnp.float32)
    wide = jnp.dot(land.astype(jnp.float32), spread, preferred_element_type=jnp.float32)
    own = iota((TH, TOKENS), 1) // TW == iota((TH, TOKENS), 0)
    line = jnp.sum(jnp.where(own, wide, 0.0), axis=0, keepdims=True)
    return jnp.broadcast_to(line, (TH, TOKENS))


def block(rows, pair, part):
    return pl.ds((2 * pair + part) * rows, rows)


def flags_at(rows, count=FLAGS):
    return pl.ds(2 * PAIRS * rows, count)


def side_rows(read, to_right, count):
    low = iota((8, LANES), 0) < HALO
    found = []
    for r in range(0, count, 2):
        at = r * TW + (TW - TH if to_right else 0)
        even, odd = read(at), read(at + TW)
        if to_right:
            found.append(jnp.where(low, pltpu.roll(even, HALO, 0), odd))
        else:
            found.append(jnp.where(low, even, pltpu.roll(odd, HALO, 0)))
    return found


def dilated_rows(source, at):
    quarter = iota((8, LANES), 0) % RATE
    found = [[] for _ in range(RATE)]
    for g in range(ROWS // 8):
        tiles = [source[pl.ds((g * RATE + i) * 8, 8), at] for i in range(RATE)]
        turned = [[t] + [pltpu.roll(t, d, 0) for d in range(1, RATE)] for t in tiles]
        for o in range(RATE):
            rows = turned[0][-o % RATE]
            for i in range(1, RATE):
                rows = jnp.where(quarter == i, turned[i][(i - o) % RATE], rows)
            found[o].append(rows)
    return [jnp.concatenate(rows, axis=0) for rows in found]


def far_token(n, o):
    i = n % RATE
    half = (n % 8) // RATE
    half = jnp.where(i < o, 1 - half, half)
    return (n // 8 * RATE + i) * 8 + o + RATE * half


def upper(step, axis="lon"):
    return lax.axis_index(axis) // step % 2


def edge_kernel(k, v, land, later, sooner, flags, sems, flags_sem):
    last = pl.multiple_of(upper(1, "lat") * (TOKENS - EDGE), EDGE)
    fetch = pltpu.make_async_copy(land, flags, flags_sem)
    fetch.start()
    copies = []
    for pair in range(PAIRS):
        for part, source in enumerate((k, v)):
            for which, (target, start) in enumerate(((later, last), (sooner, TOKENS - EDGE - last))):
                copies.append(
                    pltpu.make_async_copy(
                        source.at[pl.ds(pl.multiple_of(start, EDGE), EDGE), pl.ds(pair * LANES, LANES)],
                        target.at[block(EDGE, pair, part), :],
                        sems.at[(2 * pair + part) * 2 + which],
                    )
                )
                copies[-1].start()
    fetch.wait()
    line = land_line(flags[...])
    later[flags_at(EDGE), :] = line
    sooner[flags_at(EDGE), :] = line
    for copy in copies:
        copy.wait()


def arriving(s):
    mine = upper(2 ** (s // 2 + 1))
    return mine if s % 2 == 0 else 1 - mine


def far_kernel(offsets, k, v, land, far0, far1, far2, far3):
    line = land_line(land[...])
    first = iota((ROWS, LANES), 1) < HEAD
    fars = (far0, far1, far2, far3)
    for far in fars:
        far[flags_at(ROWS), :] = line
    for pair in range(PAIRS):
        at = pl.ds(pair * LANES, LANES)
        for part, source in enumerate((k, v)):
            rows = dilated_rows(source, at)
            for s, far in enumerate(fars):
                level, heading = s // 2, 1 - arriving(s)
                want = jnp.where(
                    first,
                    offsets[level, heading, 2 * pair],
                    offsets[level, heading, 2 * pair + 1],
                )
                picked = rows[0]
                for o in range(1, RATE):
                    picked = jnp.where(want == o, rows[o], picked)
                far[block(ROWS, pair, part), :] = picked


def side_kernel(k, v, land, later, sooner, to_cross, to_near):
    odd = upper(1) == 1
    for pair in range(PAIRS):
        at = pl.ds(pair * LANES, LANES)
        for part, own in enumerate((k, v)):
            start = (2 * pair + part) * EDGE
            both = []
            for right in (True, False):
                rows = side_rows(lambda row: own[pl.ds(row, 8), at], right, TH)
                for source in (later, sooner):
                    rows += side_rows(lambda row: source[pl.ds(start + row, 8), :], right, HALO)
                both.append(jnp.concatenate(rows, axis=0))
            to_cross[block(2 * SIDE, pair, part), :] = jnp.where(odd, both[0], both[1])
            to_near[block(2 * SIDE, pair, part), :] = jnp.where(odd, both[1], both[0])
    row = iota((FLAGS, LANES), 0)
    near = land_line(land[...])
    line = jnp.where(
        row == 0, near, jnp.where(row == 1, later[flags_at(EDGE), :], sooner[flags_at(EDGE), :])
    )
    to_cross[flags_at(2 * SIDE), :] = line
    to_near[flags_at(2 * SIDE), :] = line


def split2(x):
    high = x.astype(jnp.bfloat16)
    low = (x - high.astype(jnp.float32)).astype(jnp.bfloat16)
    return high, low


def split3(x):
    high = x.astype(jnp.bfloat16)
    rest = x - high.astype(jnp.float32)
    mid = rest.astype(jnp.bfloat16)
    low = (rest - mid.astype(jnp.float32)).astype(jnp.bfloat16)
    return high, mid, low


def spacing(row, col):
    query = iota(row.shape, 1)
    return jnp.maximum(jnp.abs(query // TW - row), jnp.abs(query % TW - col))


def across(x, y):
    return lax.dot_general(x, y, (((1,), (1,)), ((), ())), preferred_element_type=jnp.float32)


def flag_columns(line, token, lines):
    shape = (line.shape[0], LANES)
    spot = line * LANES + token - iota(shape, 1)
    pick = [(spot == at * LANES).astype(jnp.bfloat16) for at in range(len(lines))]
    rows = [jnp.broadcast_to(row, (LANES, LANES)).astype(jnp.bfloat16) for row in lines]
    return across(jnp.concatenate(pick, axis=1), jnp.concatenate(rows, axis=1))


def reach(row, col, flags):
    gap = spacing(row, col)
    return jnp.where((flags > 0.5) | (gap == 0), gap, 99)


def own_reach(land):
    key = iota((TOKENS, LANES), 0)
    return reach(key // TW, key % TW, flag_columns(key * 0, key, [land_line(land[...])[0:1]]))


def edge_reach(later, sooner):
    key = iota((2 * EDGE, LANES), 0)
    half, spot = key // EDGE, key % EDGE
    low = jnp.where(upper(1, "lat") == 1, 1 - half, half) == 1
    row = spot // TW + jnp.where(low, TH, -HALO)
    token = spot + jnp.where(low, 0, TOKENS - EDGE)
    lines = [source[flags_at(EDGE, 1), :] for source in (later, sooner)]
    return reach(row, key % TW, flag_columns(half, token, lines))


def side_reach(crossed, nearby):
    key = iota((4 * SIDE, LANES), 0)
    which, corner = key // (2 * SIDE), key // SIDE % 2
    right = jnp.where(upper(1) == 1, 1 - which, which)
    r, j = key % SIDE // HALO, key % HALO
    half = r // HALO
    low = jnp.where(upper(1, "lat") == 1, 1 - half, half) == 1
    row = jnp.where(corner == 0, r, r % HALO + jnp.where(low, TH, -HALO))
    col = jnp.where(right == 0, j - HALO, TW + j)
    token = (row + TH) % TH * TW + (col + TW) % TW
    line = 3 * which + jnp.where(corner == 0, 0, 1 + half)
    lines = []
    for source in (crossed, nearby):
        found = source[flags_at(2 * SIDE), :]
        lines += [found[i : i + 1] for i in range(3)]
    return reach(row, col, flag_columns(line, token, lines))


def far_bias(far):
    key = iota((TOKENS, LANES), 0)
    token = far_token(key % ROWS, key // ROWS)
    flags = flag_columns(key * 0, token, [far[flags_at(ROWS, 1), :]])
    return jnp.where(flags > 0.5, 0.0, -jnp.inf)


def near_bias(bias, at, found):
    for r in range(HALO):
        bias[r, pl.ds(at, found.shape[0]), :] = jnp.where(found <= r + 1, 0.0, -jnp.inf)


def twice(x):
    first = iota(x.shape, 1) < HEAD
    return jnp.concatenate([jnp.where(first, x, 0.0), jnp.where(first, 0.0, x)], axis=0)


def own_columns(x):
    return jnp.concatenate([x[:HEAD, :TOKENS], x[HEAD:, TOKENS:]], axis=0)


def over_features(x):
    return jnp.concatenate(
        [
            jnp.broadcast_to(x[:, :TOKENS], (HEAD, TOKENS)),
            jnp.broadcast_to(x[:, TOKENS:], (HEAD, TOKENS)),
        ],
        axis=0,
    )


def scores(key, query):
    q1, q2, q3 = split3(twice(query * 0.125))
    k1, k2, k3 = split3(key)
    return across(
        jnp.concatenate([k1, k2, k1, k2, k3, k1], axis=1),
        jnp.concatenate([q1, q1, q2, q2, q1, q3], axis=1),
    )


def mixture(weight, value):
    p1, p2 = split2(weight)
    v1, v2 = split2(value.T)
    ones = jnp.ones((16, weight.shape[0]), jnp.bfloat16)
    zeros = jnp.zeros((16, weight.shape[0]), jnp.bfloat16)
    v1 = jnp.concatenate([v1, ones], axis=0)
    v2 = jnp.concatenate([v2, zeros], axis=0)
    mixed = jnp.dot(
        jnp.concatenate([v1, v1, v2], axis=1),
        jnp.concatenate([p1, p2, p1], axis=0),
        preferred_element_type=jnp.float32,
    )
    return own_columns(mixed[:LANES]), mixed[LANES : LANES + 1]


def first_kernel(
    offsets, radius, q, k, v, land, later, sooner, far0, far1, far2, far3, mixed, total, peak,
    near, beyond,
):
    fars = (far0, far1, far2, far3)
    near_bias(near, 0, own_reach(land))
    near_bias(near, TOKENS, edge_reach(later, sooner))
    for s, far in enumerate(fars):
        beyond[s] = far_bias(far)

    def gather(part, pair, at):
        pieces = [(k, v)[part][:, at]]
        pieces += [source[block(EDGE, pair, part), :] for source in (later, sooner)]
        pieces += [source[block(ROWS, pair, part), :] for source in fars]
        return jnp.concatenate(pieces, axis=0)

    def barrier(pair):
        bias = []
        for head in (2 * pair, 2 * pair + 1):
            rows = [near[radius[head] - 1]]
            for s in range(4):
                start = pl.multiple_of(offsets[s // 2, arriving(s), head] * ROWS, ROWS)
                rows.append(beyond[s, pl.ds(start, ROWS), :])
            bias.append(jnp.concatenate(rows, axis=0))
        return jnp.concatenate(bias, axis=1)

    def body(pairs, ats):
        masked = [scores(gather(0, pair, at), q[:, at]) for pair, at in zip(pairs, ats)]
        masked = [x + barrier(pair) for x, pair in zip(masked, pairs)]
        tops = [jnp.max(x, axis=0, keepdims=True) for x in masked]
        weights = [jnp.exp(x - top) for x, top in zip(masked, tops)]
        mixes = [mixture(x, gather(1, *at)) for x, at in zip(weights, zip(pairs, ats))]
        for pair, at, top, (mix, weight) in zip(pairs, ats, tops, mixes):
            mixed[at, :] = mix
            total[pair] = jnp.broadcast_to(weight, (8, 2 * TOKENS))
            peak[pair] = jnp.broadcast_to(top, (8, 2 * TOKENS))

    body(range(PAIRS), [pl.ds(pair * LANES, LANES) for pair in range(PAIRS)])


def second_kernel(radius, q, crossed, nearby, mixed, total, peak, out, near):
    near_bias(near, 0, side_reach(crossed, nearby))

    def gather(part, pair):
        return jnp.concatenate(
            [source[block(2 * SIDE, pair, part), :] for source in (crossed, nearby)], axis=0
        )

    def barrier(pair):
        return jnp.concatenate([near[radius[head] - 1] for head in (2 * pair, 2 * pair + 1)], axis=1)

    def body(pairs, ats):
        masked = [scores(gather(0, pair), q[:, at]) for pair, at in zip(pairs, ats)]
        masked = [x + barrier(pair) for x, pair in zip(masked, pairs)]
        old = [peak[pair][0:1] for pair in pairs]
        tops = [jnp.maximum(jnp.max(x, axis=0, keepdims=True), y) for x, y in zip(masked, old)]
        weights = [jnp.exp(x - top) for x, top in zip(masked, tops)]
        mixes = [mixture(x, gather(1, pair)) for x, pair in zip(weights, pairs)]
        done = []
        for pair, at, top, before, (mix, weight) in zip(pairs, ats, tops, old, mixes):
            shrink = jnp.exp(before - top)
            inverse = 1.0 / (total[pair][0:1] * shrink + weight)
            done.append(
                mixed[at, :] * over_features(shrink * inverse) + mix * over_features(inverse)
            )
        for at, mix in zip(ats, done):
            out[:, at] = mix.T

    body(range(PAIRS), [pl.ds(pair * LANES, LANES) for pair in range(PAIRS)])


def swapped(value, axis, step, later, cycle=True):
    count = lax.axis_size(axis)
    pairs = []
    for source in range(count):
        ahead = source // step % 2 == (1 if later else 0)
        target = source + (step if ahead else -step)
        if cycle or 0 <= target < count:
            pairs.append((source, target % count))
    return lax.ppermute(value, axis, pairs)


def vmem(count):
    return [pl.BlockSpec(memory_space=pltpu.VMEM)] * count


def smem(count):
    return [pl.BlockSpec(memory_space=pltpu.SMEM)] * count


def payload(rows):
    return jax.ShapeDtypeStruct((2 * PAIRS * rows + FLAGS, LANES), jnp.float32)


def call(kernel, name, outs, smems, vmems, flops, moved, scratch=(), limit=16):
    return pl.pallas_call(
        kernel,
        out_shape=outs,
        in_specs=smem(smems) + vmem(vmems),
        out_specs=vmem(len(outs)),
        scratch_shapes=list(scratch),
        compiler_params=pltpu.CompilerParams(vmem_limit_bytes=limit << 20),
        cost_estimate=pl.CostEstimate(
            flops=flops, bytes_accessed=moved << 20, transcendentals=0
        ),
        name=name,
    )


def local(queries, key_vectors, value_vectors, land_mask, radius, offsets):
    q = queries.reshape(TOKENS, D)
    k = key_vectors.reshape(TOKENS, D)
    v = value_vectors.reshape(TOKENS, D)
    later, sooner = pl.pallas_call(
        edge_kernel,
        out_shape=[payload(EDGE)] * 2,
        in_specs=[pl.BlockSpec(memory_space=pltpu.HBM)] * 3,
        out_specs=vmem(2),
        scratch_shapes=[
            pltpu.VMEM((TH, TW), jnp.int32),
            pltpu.SemaphoreType.DMA((4 * PAIRS,)),
            pltpu.SemaphoreType.DMA,
        ],
        compiler_params=pltpu.CompilerParams(vmem_limit_bytes=16 << 20),
        cost_estimate=pl.CostEstimate(flops=1 << 16, bytes_accessed=2 << 20, transcendentals=0),
        name="edge",
    )(*(pltpu.with_memory_space_constraint(x, pltpu.HBM) for x in (k, v, land_mask)))
    k, v, land_mask, later, sooner = lax.optimization_barrier((k, v, land_mask, later, sooner))
    later = swapped(later, "lat", 1, True, False)
    sooner = swapped(sooner, "lat", 1, False, False)
    fars = call(far_kernel, "far", [payload(ROWS)] * 4, 1, 3, 1 << 20, 2)(
        offsets, k, v, land_mask
    )
    fars, arrived = list(fars), [None] * 4
    for s in (0, 2, 1, 3):
        if s == 3:
            arrived[2], fars[3] = lax.optimization_barrier((arrived[2], fars[3]))
        arrived[s] = swapped(fars[s], "lon", 2 ** (s // 2 + 1), s % 2 == 1)
    to_cross, to_near = call(
        side_kernel, "side", [payload(2 * SIDE)] * 2, 0, 5, 1 << 33, 3
    )(k, v, land_mask, later, sooner)
    crossed = swapped(to_cross, "lon", 1, True)
    nearby = swapped(to_near, "lon", 1, False)
    line = jax.ShapeDtypeStruct((PAIRS, 8, 2 * TOKENS), jnp.float32)
    partial = call(
        first_kernel, "first", [jax.ShapeDtypeStruct((D, TOKENS), jnp.float32), line, line],
        2, 10, 1 << 34, 6,
        [
            pltpu.VMEM((HALO, 2 * TOKENS, LANES), jnp.float32),
            pltpu.VMEM((4, TOKENS, LANES), jnp.float32),
        ],
        24,
    )(offsets, radius, q, k, v, land_mask, later, sooner, *arrived)
    [result] = call(
        second_kernel, "second", [jax.ShapeDtypeStruct((TOKENS, D), jnp.float32)],
        1, 6, 1 << 28, 4, [pltpu.VMEM((HALO, TOKENS, LANES), jnp.float32)],
    )(radius, q, crossed, nearby, *partial)
    return result.reshape(TH, TW, D)


def solution(mesh):
    tile = P("lat", "lon", None)
    in_specs = (tile, tile, tile, P("lat", "lon"), P(), P())
    return jax.shard_map(local, mesh=mesh, in_specs=in_specs, out_specs=tile, check_vma=False)
```

```python
import functools

import jax
import jax.numpy as jnp
from jax import lax
from jax.experimental import pallas as pl
from jax.experimental.pallas import tpu as pltpu
from jax.sharding import PartitionSpec as P

TH = 8
TW = 16
TOKENS = TH * TW
HALO = 4
RATE = 4
LEVELS = 2
HEADS = 16
D = 1024
HEAD = D // HEADS
LANES = 128
PAIRS = D // LANES
ROWS = TOKENS // RATE
SIDE = TH * HALO
EDGE = TW * HALO
FLAGS = 8


def iota(shape, dim):
    return lax.broadcasted_iota(jnp.int32, shape, dim)


def land_line(land):
    spread = (iota((TW, TOKENS), 1) % TW == iota((TW, TOKENS), 0)).astype(jnp.float32)
    wide = jnp.dot(land.astype(jnp.float32), spread, preferred_element_type=jnp.float32)
    own = iota((TH, TOKENS), 1) // TW == iota((TH, TOKENS), 0)
    line = jnp.sum(jnp.where(own, wide, 0.0), axis=0, keepdims=True)
    return jnp.broadcast_to(line, (TH, TOKENS))


def block(rows, pair, part):
    return pl.ds((2 * pair + part) * rows, rows)


def flags_at(rows, count=FLAGS):
    return pl.ds(2 * PAIRS * rows, count)


def side_rows(read, to_right, count):
    low = iota((8, LANES), 0) < HALO
    found = []
    for r in range(0, count, 2):
        at = r * TW + (TW - TH if to_right else 0)
        even, odd = read(at), read(at + TW)
        if to_right:
            found.append(jnp.where(low, pltpu.roll(even, HALO, 0), odd))
        else:
            found.append(jnp.where(low, even, pltpu.roll(odd, HALO, 0)))
    return found


def dilated_rows(source, at):
    quarter = iota((8, LANES), 0) % RATE
    found = [[] for _ in range(RATE)]
    for g in range(ROWS // 8):
        tiles = [source[pl.ds((g * RATE + i) * 8, 8), at] for i in range(RATE)]
        turned = [[t] + [pltpu.roll(t, d, 0) for d in range(1, RATE)] for t in tiles]
        for o in range(RATE):
            rows = turned[0][-o % RATE]
            for i in range(1, RATE):
                rows = jnp.where(quarter == i, turned[i][(i - o) % RATE], rows)
            found[o].append(rows)
    return [jnp.concatenate(rows, axis=0) for rows in found]


def far_token(n, o):
    i = n % RATE
    half = (n % 8) // RATE
    half = jnp.where(i < o, 1 - half, half)
    return (n // 8 * RATE + i) * 8 + o + RATE * half


def upper(step, axis="lon"):
    return lax.axis_index(axis) // step % 2


def edge_kernel(k, v, land, later, sooner, flags, sems, flags_sem):
    last = pl.multiple_of(upper(1, "lat") * (TOKENS - EDGE), EDGE)
    fetch = pltpu.make_async_copy(land, flags, flags_sem)
    fetch.start()
    copies = []
    for pair in range(PAIRS):
        for part, source in enumerate((k, v)):
            for which, (target, start) in enumerate(((later, last), (sooner, TOKENS - EDGE - last))):
                copies.append(
                    pltpu.make_async_copy(
                        source.at[pl.ds(pl.multiple_of(start, EDGE), EDGE), pl.ds(pair * LANES, LANES)],
                        target.at[block(EDGE, pair, part), :],
                        sems.at[(2 * pair + part) * 2 + which],
                    )
                )
                copies[-1].start()
    fetch.wait()
    line = land_line(flags[...])
    later[flags_at(EDGE), :] = line
    sooner[flags_at(EDGE), :] = line
    for copy in copies:
        copy.wait()


def arriving(s):
    mine = upper(2 ** (s // 2 + 1))
    return mine if s % 2 == 0 else 1 - mine


def far_kernel(offsets, k, v, land, far0, far1, far2, far3):
    line = land_line(land[...])
    first = iota((ROWS, LANES), 1) < HEAD
    fars = (far0, far1, far2, far3)
    for far in fars:
        far[flags_at(ROWS), :] = line
    for pair in range(PAIRS):
        at = pl.ds(pair * LANES, LANES)
        for part, source in enumerate((k, v)):
            rows = dilated_rows(source, at)
            for s, far in enumerate(fars):
                level, heading = s // 2, 1 - arriving(s)
                want = jnp.where(
                    first,
                    offsets[level, heading, 2 * pair],
                    offsets[level, heading, 2 * pair + 1],
                )
                picked = rows[0]
                for o in range(1, RATE):
                    picked = jnp.where(want == o, rows[o], picked)
                far[block(ROWS, pair, part), :] = picked


def side_kernel(k, v, land, later, sooner, to_cross, to_near):
    odd = upper(1) == 1
    for pair in range(PAIRS):
        at = pl.ds(pair * LANES, LANES)
        for part, own in enumerate((k, v)):
            start = (2 * pair + part) * EDGE
            both = []
            for right in (True, False):
                rows = side_rows(lambda row: own[pl.ds(row, 8), at], right, TH)
                for source in (later, sooner):
                    rows += side_rows(lambda row: source[pl.ds(start + row, 8), :], right, HALO)
                both.append(jnp.concatenate(rows, axis=0))
            to_cross[block(2 * SIDE, pair, part), :] = jnp.where(odd, both[0], both[1])
            to_near[block(2 * SIDE, pair, part), :] = jnp.where(odd, both[1], both[0])
    row = iota((FLAGS, LANES), 0)
    near = land_line(land[...])
    line = jnp.where(
        row == 0, near, jnp.where(row == 1, later[flags_at(EDGE), :], sooner[flags_at(EDGE), :])
    )
    to_cross[flags_at(2 * SIDE), :] = line
    to_near[flags_at(2 * SIDE), :] = line


def split2(x):
    high = x.astype(jnp.bfloat16)
    low = (x - high.astype(jnp.float32)).astype(jnp.bfloat16)
    return high, low


def split3(x):
    high = x.astype(jnp.bfloat16)
    rest = x - high.astype(jnp.float32)
    mid = rest.astype(jnp.bfloat16)
    low = (rest - mid.astype(jnp.float32)).astype(jnp.bfloat16)
    return high, mid, low


def spacing(row, col):
    query = iota(row.shape, 1)
    return jnp.maximum(jnp.abs(query // TW - row), jnp.abs(query % TW - col))


def across(x, y):
    return lax.dot_general(x, y, (((1,), (1,)), ((), ())), preferred_element_type=jnp.float32)


def flag_columns(line, token, lines):
    shape = (line.shape[0], LANES)
    spot = line * LANES + token - iota(shape, 1)
    pick = [(spot == at * LANES).astype(jnp.bfloat16) for at in range(len(lines))]
    rows = [jnp.broadcast_to(row, (LANES, LANES)).astype(jnp.bfloat16) for row in lines]
    return across(jnp.concatenate(pick, axis=1), jnp.concatenate(rows, axis=1))


def reach(row, col, flags):
    gap = spacing(row, col)
    return jnp.where((flags > 0.5) | (gap == 0), gap, 99)


def own_reach(land):
    key = iota((TOKENS, LANES), 0)
    return reach(key // TW, key % TW, flag_columns(key * 0, key, [land_line(land[...])[0:1]]))


def edge_reach(later, sooner):
    key = iota((2 * EDGE, LANES), 0)
    half, spot = key // EDGE, key % EDGE
    low = jnp.where(upper(1, "lat") == 1, 1 - half, half) == 1
    row = spot // TW + jnp.where(low, TH, -HALO)
    token = spot + jnp.where(low, 0, TOKENS - EDGE)
    lines = [source[flags_at(EDGE, 1), :] for source in (later, sooner)]
    return reach(row, key % TW, flag_columns(half, token, lines))


def side_reach(crossed, nearby):
    key = iota((4 * SIDE, LANES), 0)
    which, corner = key // (2 * SIDE), key // SIDE % 2
    right = jnp.where(upper(1) == 1, 1 - which, which)
    r, j = key % SIDE // HALO, key % HALO
    half = r // HALO
    low = jnp.where(upper(1, "lat") == 1, 1 - half, half) == 1
    row = jnp.where(corner == 0, r, r % HALO + jnp.where(low, TH, -HALO))
    col = jnp.where(right == 0, j - HALO, TW + j)
    token = (row + TH) % TH * TW + (col + TW) % TW
    line = 3 * which + jnp.where(corner == 0, 0, 1 + half)
    lines = []
    for source in (crossed, nearby):
        found = source[flags_at(2 * SIDE), :]
        lines += [found[i : i + 1] for i in range(3)]
    return reach(row, col, flag_columns(line, token, lines))


def far_bias(far):
    key = iota((TOKENS, LANES), 0)
    token = far_token(key % ROWS, key // ROWS)
    flags = flag_columns(key * 0, token, [far[flags_at(ROWS, 1), :]])
    return jnp.where(flags > 0.5, 0.0, -jnp.inf)


def near_bias(bias, at, found):
    for r in range(HALO):
        bias[r, pl.ds(at, found.shape[0]), :] = jnp.where(found <= r + 1, 0.0, -jnp.inf)


def twice(x):
    first = iota(x.shape, 1) < HEAD
    return jnp.concatenate([jnp.where(first, x, 0.0), jnp.where(first, 0.0, x)], axis=0)


def own_columns(x):
    return jnp.concatenate([x[:HEAD, :TOKENS], x[HEAD:, TOKENS:]], axis=0)


def over_features(x):
    return jnp.concatenate(
        [
            jnp.broadcast_to(x[:, :TOKENS], (HEAD, TOKENS)),
            jnp.broadcast_to(x[:, TOKENS:], (HEAD, TOKENS)),
        ],
        axis=0,
    )


def scores(key, query):
    q1, q2, q3 = split3(twice(query * 0.125))
    k1, k2, k3 = split3(key)
    return across(
        jnp.concatenate([k1, k2, k1, k2, k3, k1], axis=1),
        jnp.concatenate([q1, q1, q2, q2, q1, q3], axis=1),
    )


def few_scores(key, query):
    keys = key.shape[0]
    q1, q2, q3 = split3(twice(query * 0.125))
    k1, k2, k3 = split3(key)
    rows = jnp.concatenate([k1, k2, k3], axis=0)
    beside = jnp.concatenate([k1, k2, jnp.zeros_like(k3)], axis=0)
    found = across(
        jnp.concatenate([rows, beside], axis=1), jnp.concatenate([q1, q2], axis=1)
    )
    rest = found[keys : 2 * keys] + (found[2 * keys :] + across(k1, q3))
    return found[:keys] + rest


def mixture(weight, value):
    p1, p2 = split2(weight)
    v1, v2 = split2(value.T)
    ones = jnp.ones((16, weight.shape[0]), jnp.bfloat16)
    zeros = jnp.zeros((16, weight.shape[0]), jnp.bfloat16)
    v1 = jnp.concatenate([v1, ones], axis=0)
    v2 = jnp.concatenate([v2, zeros], axis=0)
    mixed = jnp.dot(
        jnp.concatenate([v1, v1, v2], axis=1),
        jnp.concatenate([p1, p2, p1], axis=0),
        preferred_element_type=jnp.float32,
    )
    return own_columns(mixed[:LANES]), mixed[LANES : LANES + 1]


def first_kernel(
    offsets, radius, q, k, v, land, later, sooner, far0, far1, far2, far3, mixed, total, peak,
    near, beyond,
):
    fars = (far0, far1, far2, far3)
    near_bias(near, 0, own_reach(land))
    near_bias(near, TOKENS, edge_reach(later, sooner))
    for s, far in enumerate(fars):
        beyond[s] = far_bias(far)

    def gather(part, pair, at):
        pieces = [(k, v)[part][:, at]]
        pieces += [source[block(EDGE, pair, part), :] for source in (later, sooner)]
        pieces += [source[block(ROWS, pair, part), :] for source in fars]
        return jnp.concatenate(pieces, axis=0)

    def barrier(pair):
        bias = []
        for head in (2 * pair, 2 * pair + 1):
            rows = [near[radius[head] - 1]]
            for s in range(4):
                start = pl.multiple_of(offsets[s // 2, arriving(s), head] * ROWS, ROWS)
                rows.append(beyond[s, pl.ds(start, ROWS), :])
            bias.append(jnp.concatenate(rows, axis=0))
        return jnp.concatenate(bias, axis=1)

    def body(pairs, ats):
        masked = [scores(gather(0, pair, at), q[:, at]) for pair, at in zip(pairs, ats)]
        masked = [x + barrier(pair) for x, pair in zip(masked, pairs)]
        tops = [jnp.max(x, axis=0, keepdims=True) for x in masked]
        weights = [jnp.exp(x - top) for x, top in zip(masked, tops)]
        mixes = [mixture(x, gather(1, *at)) for x, at in zip(weights, zip(pairs, ats))]
        for pair, at, top, (mix, weight) in zip(pairs, ats, tops, mixes):
            mixed[at, :] = mix
            total[pair] = jnp.broadcast_to(weight, (8, 2 * TOKENS))
            peak[pair] = jnp.broadcast_to(top, (8, 2 * TOKENS))

    body(range(PAIRS), [pl.ds(pair * LANES, LANES) for pair in range(PAIRS)])


def second_kernel(radius, q, crossed, nearby, mixed, total, peak, out, near, tile, sems):
    near_bias(near, 0, side_reach(crossed, nearby))

    def gather(part, pair):
        return jnp.concatenate(
            [source[block(2 * SIDE, pair, part), :] for source in (crossed, nearby)], axis=0
        )

    def barrier(pair):
        return jnp.concatenate([near[radius[head] - 1] for head in (2 * pair, 2 * pair + 1)], axis=1)

    def body(pairs, ats):
        masked = [few_scores(gather(0, pair), q[:, at]) for pair, at in zip(pairs, ats)]
        masked = [x + barrier(pair) for x, pair in zip(masked, pairs)]
        old = [peak[pair][0:1] for pair in pairs]
        tops = [jnp.maximum(jnp.max(x, axis=0, keepdims=True), y) for x, y in zip(masked, old)]
        weights = [jnp.exp(x - top) for x, top in zip(masked, tops)]
        mixes = [mixture(x, gather(1, pair)) for x, pair in zip(weights, pairs)]
        done = []
        for pair, at, top, before, (mix, weight) in zip(pairs, ats, tops, old, mixes):
            shrink = jnp.exp(before - top)
            inverse = 1.0 / (total[pair][0:1] * shrink + weight)
            done.append(
                mixed[at, :] * over_features(shrink * inverse) + mix * over_features(inverse)
            )
        copies = []
        for pair, at, mix in zip(pairs, ats, done):
            tile[:, at] = mix.T
            copies.append(pltpu.make_async_copy(tile.at[:, at], out.at[:, at], sems.at[pair]))
            copies[-1].start()
        for copy in copies:
            copy.wait()

    body(range(PAIRS), [pl.ds(pair * LANES, LANES) for pair in range(PAIRS)])


def swapped(value, axis, step, later, cycle=True):
    count = lax.axis_size(axis)
    pairs = []
    for source in range(count):
        ahead = source // step % 2 == (1 if later else 0)
        target = source + (step if ahead else -step)
        if cycle or 0 <= target < count:
            pairs.append((source, target % count))
    return lax.ppermute(value, axis, pairs)


def vmem(count):
    return [pl.BlockSpec(memory_space=pltpu.VMEM)] * count


def smem(count):
    return [pl.BlockSpec(memory_space=pltpu.SMEM)] * count


def payload(rows):
    return jax.ShapeDtypeStruct((2 * PAIRS * rows + FLAGS, LANES), jnp.float32)


def call(kernel, name, outs, smems, vmems, flops, moved, scratch=(), limit=16):
    return pl.pallas_call(
        kernel,
        out_shape=outs,
        in_specs=smem(smems) + vmem(vmems),
        out_specs=vmem(len(outs)),
        scratch_shapes=list(scratch),
        compiler_params=pltpu.CompilerParams(vmem_limit_bytes=limit << 20),
        cost_estimate=pl.CostEstimate(
            flops=flops, bytes_accessed=moved << 20, transcendentals=0
        ),
        name=name,
    )


def local(queries, key_vectors, value_vectors, land_mask, radius, offsets):
    q = queries.reshape(TOKENS, D)
    k = key_vectors.reshape(TOKENS, D)
    v = value_vectors.reshape(TOKENS, D)
    later, sooner = pl.pallas_call(
        edge_kernel,
        out_shape=[payload(EDGE)] * 2,
        in_specs=[pl.BlockSpec(memory_space=pltpu.HBM)] * 3,
        out_specs=vmem(2),
        scratch_shapes=[
            pltpu.VMEM((TH, TW), jnp.int32),
            pltpu.SemaphoreType.DMA((4 * PAIRS,)),
            pltpu.SemaphoreType.DMA,
        ],
        compiler_params=pltpu.CompilerParams(vmem_limit_bytes=16 << 20),
        cost_estimate=pl.CostEstimate(flops=1 << 16, bytes_accessed=2 << 20, transcendentals=0),
        name="edge",
    )(*(pltpu.with_memory_space_constraint(x, pltpu.HBM) for x in (k, v, land_mask)))
    k, v, land_mask, later, sooner = lax.optimization_barrier((k, v, land_mask, later, sooner))
    later = swapped(later, "lat", 1, True, False)
    sooner = swapped(sooner, "lat", 1, False, False)
    fars = call(far_kernel, "far", [payload(ROWS)] * 4, 1, 3, 1 << 20, 2)(
        offsets, k, v, land_mask
    )
    fars, arrived = list(fars), [None] * 4
    for s in (0, 2, 1, 3):
        if s == 3:
            arrived[2], fars[3] = lax.optimization_barrier((arrived[2], fars[3]))
        arrived[s] = swapped(fars[s], "lon", 2 ** (s // 2 + 1), s % 2 == 1)
    to_cross, to_near = call(
        side_kernel, "side", [payload(2 * SIDE)] * 2, 0, 5, 1 << 33, 3
    )(k, v, land_mask, later, sooner)
    crossed = swapped(to_cross, "lon", 1, True)
    nearby = swapped(to_near, "lon", 1, False)
    line = jax.ShapeDtypeStruct((PAIRS, 8, 2 * TOKENS), jnp.float32)
    partial = call(
        first_kernel, "first", [jax.ShapeDtypeStruct((D, TOKENS), jnp.float32), line, line],
        2, 10, 1 << 34, 6,
        [
            pltpu.VMEM((HALO, 2 * TOKENS, LANES), jnp.float32),
            pltpu.VMEM((4, TOKENS, LANES), jnp.float32),
        ],
        24,
    )(offsets, radius, q, k, v, land_mask, later, sooner, *arrived)
    result = pl.pallas_call(
        second_kernel,
        out_shape=jax.ShapeDtypeStruct((TOKENS, D), jnp.float32),
        in_specs=smem(1) + vmem(6),
        out_specs=pl.BlockSpec(memory_space=pltpu.HBM),
        scratch_shapes=[
            pltpu.VMEM((HALO, TOKENS, LANES), jnp.float32),
            pltpu.VMEM((TOKENS, D), jnp.float32),
            pltpu.SemaphoreType.DMA((PAIRS,)),
        ],
        compiler_params=pltpu.CompilerParams(vmem_limit_bytes=16 << 20),
        cost_estimate=pl.CostEstimate(flops=1 << 28, bytes_accessed=4 << 20, transcendentals=0),
        name="second",
    )(radius, q, crossed, nearby, *partial)
    return result.reshape(TH, TW, D)


def solution(mesh):
    tile = P("lat", "lon", None)
    in_specs = (tile, tile, tile, P("lat", "lon"), P(), P())
    return jax.shard_map(local, mesh=mesh, in_specs=in_specs, out_specs=tile, check_vma=False)
```

```python
import functools

import jax
import jax.numpy as jnp
from jax import lax
from jax.experimental import pallas as pl
from jax.experimental.pallas import tpu as pltpu
from jax.sharding import PartitionSpec as P

TH = 8
TW = 16
TOKENS = TH * TW
HALO = 4
RATE = 4
LEVELS = 2
HEADS = 16
D = 1024
HEAD = D // HEADS
LANES = 128
PAIRS = D // LANES
ROWS = TOKENS // RATE
SIDE = TH * HALO
EDGE = TW * HALO
FLAGS = 8


def iota(shape, dim):
    return lax.broadcasted_iota(jnp.int32, shape, dim)


def land_line(land):
    spread = (iota((TW, TOKENS), 1) % TW == iota((TW, TOKENS), 0)).astype(jnp.float32)
    wide = jnp.dot(land.astype(jnp.float32), spread, preferred_element_type=jnp.float32)
    own = iota((TH, TOKENS), 1) // TW == iota((TH, TOKENS), 0)
    line = jnp.sum(jnp.where(own, wide, 0.0), axis=0, keepdims=True)
    return jnp.broadcast_to(line, (TH, TOKENS))


def block(rows, pair, part):
    return pl.ds((2 * pair + part) * rows, rows)


def flags_at(rows, count=FLAGS):
    return pl.ds(2 * PAIRS * rows, count)


def side_rows(read, to_right, count):
    low = iota((8, LANES), 0) < HALO
    found = []
    for r in range(0, count, 2):
        at = r * TW + (TW - TH if to_right else 0)
        even, odd = read(at), read(at + TW)
        if to_right:
            found.append(jnp.where(low, pltpu.roll(even, HALO, 0), odd))
        else:
            found.append(jnp.where(low, even, pltpu.roll(odd, HALO, 0)))
    return found


def dilated_rows(source, at):
    quarter = iota((8, LANES), 0) % RATE
    found = [[] for _ in range(RATE)]
    for g in range(ROWS // 8):
        tiles = [source[pl.ds((g * RATE + i) * 8, 8), at] for i in range(RATE)]
        turned = [[t] + [pltpu.roll(t, d, 0) for d in range(1, RATE)] for t in tiles]
        for o in range(RATE):
            rows = turned[0][-o % RATE]
            for i in range(1, RATE):
                rows = jnp.where(quarter == i, turned[i][(i - o) % RATE], rows)
            found[o].append(rows)
    return [jnp.concatenate(rows, axis=0) for rows in found]


def far_token(n, o):
    i = n % RATE
    half = (n % 8) // RATE
    half = jnp.where(i < o, 1 - half, half)
    return (n // 8 * RATE + i) * 8 + o + RATE * half


def upper(step, axis="lon"):
    return lax.axis_index(axis) // step % 2


def edge_kernel(k, v, land, later, sooner, flags, sems, flags_sem):
    last = pl.multiple_of(upper(1, "lat") * (TOKENS - EDGE), EDGE)
    fetch = pltpu.make_async_copy(land, flags, flags_sem)
    fetch.start()
    copies = []
    for pair in range(PAIRS):
        for part, source in enumerate((k, v)):
            for which, (target, start) in enumerate(((later, last), (sooner, TOKENS - EDGE - last))):
                copies.append(
                    pltpu.make_async_copy(
                        source.at[pl.ds(pl.multiple_of(start, EDGE), EDGE), pl.ds(pair * LANES, LANES)],
                        target.at[block(EDGE, pair, part), :],
                        sems.at[(2 * pair + part) * 2 + which],
                    )
                )
                copies[-1].start()
    fetch.wait()
    line = land_line(flags[...])
    later[flags_at(EDGE), :] = line
    sooner[flags_at(EDGE), :] = line
    for copy in copies:
        copy.wait()


def arriving(s):
    mine = upper(2 ** (s // 2 + 1))
    return mine if s % 2 == 0 else 1 - mine


def far_kernel(offsets, k, v, land, far0, far1, far2, far3):
    line = land_line(land[...])
    first = iota((ROWS, LANES), 1) < HEAD
    fars = (far0, far1, far2, far3)
    for far in fars:
        far[flags_at(ROWS), :] = line
    for pair in range(PAIRS):
        at = pl.ds(pair * LANES, LANES)
        for part, source in enumerate((k, v)):
            rows = dilated_rows(source, at)
            for s, far in enumerate(fars):
                level, heading = s // 2, 1 - arriving(s)
                want = jnp.where(
                    first,
                    offsets[level, heading, 2 * pair],
                    offsets[level, heading, 2 * pair + 1],
                )
                picked = rows[0]
                for o in range(1, RATE):
                    picked = jnp.where(want == o, rows[o], picked)
                far[block(ROWS, pair, part), :] = picked


def side_kernel(k, v, land, later, sooner, to_cross, to_near):
    odd = upper(1) == 1
    for pair in range(PAIRS):
        at = pl.ds(pair * LANES, LANES)
        for part, own in enumerate((k, v)):
            start = (2 * pair + part) * EDGE
            both = []
            for right in (True, False):
                rows = side_rows(lambda row: own[pl.ds(row, 8), at], right, TH)
                for source in (later, sooner):
                    rows += side_rows(lambda row: source[pl.ds(start + row, 8), :], right, HALO)
                both.append(jnp.concatenate(rows, axis=0))
            to_cross[block(2 * SIDE, pair, part), :] = jnp.where(odd, both[0], both[1])
            to_near[block(2 * SIDE, pair, part), :] = jnp.where(odd, both[1], both[0])
    row = iota((FLAGS, LANES), 0)
    near = land_line(land[...])
    line = jnp.where(
        row == 0, near, jnp.where(row == 1, later[flags_at(EDGE), :], sooner[flags_at(EDGE), :])
    )
    to_cross[flags_at(2 * SIDE), :] = line
    to_near[flags_at(2 * SIDE), :] = line


def split2(x):
    high = x.astype(jnp.bfloat16)
    low = (x - high.astype(jnp.float32)).astype(jnp.bfloat16)
    return high, low


def split3(x):
    high = x.astype(jnp.bfloat16)
    rest = x - high.astype(jnp.float32)
    mid = rest.astype(jnp.bfloat16)
    low = (rest - mid.astype(jnp.float32)).astype(jnp.bfloat16)
    return high, mid, low


def spacing(row, col):
    query = iota(row.shape, 1)
    return jnp.maximum(jnp.abs(query // TW - row), jnp.abs(query % TW - col))


def across(x, y):
    return lax.dot_general(x, y, (((1,), (1,)), ((), ())), preferred_element_type=jnp.float32)


def flag_columns(line, token, lines):
    shape = (line.shape[0], LANES)
    spot = line * LANES + token - iota(shape, 1)
    pick = [(spot == at * LANES).astype(jnp.bfloat16) for at in range(len(lines))]
    rows = [jnp.broadcast_to(row, (LANES, LANES)).astype(jnp.bfloat16) for row in lines]
    return across(jnp.concatenate(pick, axis=1), jnp.concatenate(rows, axis=1))


def reach(row, col, flags):
    gap = spacing(row, col)
    return jnp.where((flags > 0.5) | (gap == 0), gap, 99)


def own_reach(land):
    key = iota((TOKENS, LANES), 0)
    return reach(key // TW, key % TW, flag_columns(key * 0, key, [land_line(land[...])[0:1]]))


def edge_reach(later, sooner):
    key = iota((2 * EDGE, LANES), 0)
    half, spot = key // EDGE, key % EDGE
    low = jnp.where(upper(1, "lat") == 1, 1 - half, half) == 1
    row = spot // TW + jnp.where(low, TH, -HALO)
    token = spot + jnp.where(low, 0, TOKENS - EDGE)
    lines = [source[flags_at(EDGE, 1), :] for source in (later, sooner)]
    return reach(row, key % TW, flag_columns(half, token, lines))


def side_reach(crossed, nearby):
    key = iota((4 * SIDE, LANES), 0)
    which, corner = key // (2 * SIDE), key // SIDE % 2
    right = jnp.where(upper(1) == 1, 1 - which, which)
    r, j = key % SIDE // HALO, key % HALO
    half = r // HALO
    low = jnp.where(upper(1, "lat") == 1, 1 - half, half) == 1
    row = jnp.where(corner == 0, r, r % HALO + jnp.where(low, TH, -HALO))
    col = jnp.where(right == 0, j - HALO, TW + j)
    token = (row + TH) % TH * TW + (col + TW) % TW
    line = 3 * which + jnp.where(corner == 0, 0, 1 + half)
    lines = []
    for source in (crossed, nearby):
        found = source[flags_at(2 * SIDE), :]
        lines += [found[i : i + 1] for i in range(3)]
    return reach(row, col, flag_columns(line, token, lines))


def far_bias(far):
    key = iota((TOKENS, LANES), 0)
    token = far_token(key % ROWS, key // ROWS)
    flags = flag_columns(key * 0, token, [far[flags_at(ROWS, 1), :]])
    return jnp.where(flags > 0.5, 0.0, -jnp.inf)


def near_bias(bias, at, found):
    for r in range(HALO):
        bias[r, pl.ds(at, found.shape[0]), :] = jnp.where(found <= r + 1, 0.0, -jnp.inf)


def twice(x):
    first = iota(x.shape, 1) < HEAD
    return jnp.concatenate([jnp.where(first, x, 0.0), jnp.where(first, 0.0, x)], axis=0)


def own_columns(x):
    return jnp.concatenate([x[:HEAD, :TOKENS], x[HEAD:, TOKENS:]], axis=0)


def over_features(x):
    return jnp.concatenate(
        [
            jnp.broadcast_to(x[:, :TOKENS], (HEAD, TOKENS)),
            jnp.broadcast_to(x[:, TOKENS:], (HEAD, TOKENS)),
        ],
        axis=0,
    )


def scores(key, query):
    q1, q2, q3 = split3(twice(query * 0.125))
    k1, k2, k3 = split3(key)
    return across(
        jnp.concatenate([k1, k2, k1, k2, k3, k1], axis=1),
        jnp.concatenate([q1, q1, q2, q2, q1, q3], axis=1),
    )


def few_scores(key, query):
    keys = key.shape[0]
    q1, q2, q3 = split3(twice(query * 0.125))
    k1, k2, k3 = split3(key)
    rows = jnp.concatenate([k1, k2, k3], axis=0)
    beside = jnp.concatenate([k1, k2, jnp.zeros_like(k3)], axis=0)
    found = across(
        jnp.concatenate([rows, beside], axis=1), jnp.concatenate([q1, q2], axis=1)
    )
    rest = found[keys : 2 * keys] + (found[2 * keys :] + across(k1, q3))
    return found[:keys] + rest


def mixture(weight, value):
    p1, p2 = split2(weight)
    v1, v2 = split2(value.T)
    ones = jnp.ones((16, weight.shape[0]), jnp.bfloat16)
    zeros = jnp.zeros((16, weight.shape[0]), jnp.bfloat16)
    v1 = jnp.concatenate([v1, ones], axis=0)
    v2 = jnp.concatenate([v2, zeros], axis=0)
    mixed = jnp.dot(
        jnp.concatenate([v1, v1, v2], axis=1),
        jnp.concatenate([p1, p2, p1], axis=0),
        preferred_element_type=jnp.float32,
    )
    return own_columns(mixed[:LANES]), mixed[LANES : LANES + 1]


def first_kernel(
    offsets, radius, q, k, v, land, later, sooner, far0, far1, far2, far3, mixed, total, peak,
    near, beyond,
):
    fars = (far0, far1, far2, far3)
    near_bias(near, 0, own_reach(land))
    near_bias(near, TOKENS, edge_reach(later, sooner))
    for s, far in enumerate(fars):
        beyond[s] = far_bias(far)

    def gather(part, pair, at):
        pieces = [(k, v)[part][:, at]]
        pieces += [source[block(EDGE, pair, part), :] for source in (later, sooner)]
        pieces += [source[block(ROWS, pair, part), :] for source in fars]
        return jnp.concatenate(pieces, axis=0)

    def barrier(pair):
        bias = []
        for head in (2 * pair, 2 * pair + 1):
            rows = [near[radius[head] - 1]]
            for s in range(4):
                start = pl.multiple_of(offsets[s // 2, arriving(s), head] * ROWS, ROWS)
                rows.append(beyond[s, pl.ds(start, ROWS), :])
            bias.append(jnp.concatenate(rows, axis=0))
        return jnp.concatenate(bias, axis=1)

    def body(pairs, ats):
        masked = [scores(gather(0, pair, at), q[:, at]) for pair, at in zip(pairs, ats)]
        masked = [x + barrier(pair) for x, pair in zip(masked, pairs)]
        tops = [jnp.max(x, axis=0, keepdims=True) for x in masked]
        weights = [jnp.exp(x - top) for x, top in zip(masked, tops)]
        mixes = [mixture(x, gather(1, *at)) for x, at in zip(weights, zip(pairs, ats))]
        for pair, at, top, (mix, weight) in zip(pairs, ats, tops, mixes):
            mixed[at, :] = mix
            total[pair] = jnp.broadcast_to(weight, (8, 2 * TOKENS))
            peak[pair] = jnp.broadcast_to(top, (8, 2 * TOKENS))

    body(range(PAIRS), [pl.ds(pair * LANES, LANES) for pair in range(PAIRS)])


def second_kernel(radius, q, crossed, nearby, mixed, total, peak, out, near, tile, sems):
    near_bias(near, 0, side_reach(crossed, nearby))

    def gather(part, pair):
        return jnp.concatenate(
            [source[block(2 * SIDE, pair, part), :] for source in (crossed, nearby)], axis=0
        )

    def barrier(pair):
        return jnp.concatenate([near[radius[head] - 1] for head in (2 * pair, 2 * pair + 1)], axis=1)

    def body(pairs, ats):
        masked = [few_scores(gather(0, pair), q[:, at]) for pair, at in zip(pairs, ats)]
        masked = [x + barrier(pair) for x, pair in zip(masked, pairs)]
        old = [peak[pair][0:1] for pair in pairs]
        tops = [jnp.maximum(jnp.max(x, axis=0, keepdims=True), y) for x, y in zip(masked, old)]
        weights = [jnp.exp(x - top) for x, top in zip(masked, tops)]
        mixes = [mixture(x, gather(1, pair)) for x, pair in zip(weights, pairs)]
        done = []
        for pair, at, top, before, (mix, weight) in zip(pairs, ats, tops, old, mixes):
            shrink = jnp.exp(before - top)
            inverse = 1.0 / (total[pair][0:1] * shrink + weight)
            done.append(
                mixed[at, :] * over_features(shrink * inverse) + mix * over_features(inverse)
            )
        copies = []
        for pair, at, mix in zip(pairs, ats, done):
            tile[:, at] = mix.T
            copies.append(pltpu.make_async_copy(tile.at[:, at], out.at[:, at], sems.at[pair]))
            copies[-1].start()
        for copy in copies:
            copy.wait()

    body(range(PAIRS), [pl.ds(pair * LANES, LANES) for pair in range(PAIRS)])


def swapped(value, axis, step, later, cycle=True):
    count = lax.axis_size(axis)
    pairs = []
    for source in range(count):
        ahead = source // step % 2 == (1 if later else 0)
        target = source + (step if ahead else -step)
        if cycle or 0 <= target < count:
            pairs.append((source, target % count))
    return lax.ppermute(value, axis, pairs)


def vmem(count):
    return [pl.BlockSpec(memory_space=pltpu.VMEM)] * count


def smem(count):
    return [pl.BlockSpec(memory_space=pltpu.SMEM)] * count


def payload(rows):
    return jax.ShapeDtypeStruct((2 * PAIRS * rows + FLAGS, LANES), jnp.float32)


def call(kernel, name, outs, smems, vmems, flops, moved, scratch=(), limit=16):
    return pl.pallas_call(
        kernel,
        out_shape=outs,
        in_specs=smem(smems) + vmem(vmems),
        out_specs=vmem(len(outs)),
        scratch_shapes=list(scratch),
        compiler_params=pltpu.CompilerParams(vmem_limit_bytes=limit << 20),
        cost_estimate=pl.CostEstimate(
            flops=flops, bytes_accessed=moved << 20, transcendentals=0
        ),
        name=name,
    )


def local(queries, key_vectors, value_vectors, land_mask, radius, offsets):
    q = queries.reshape(TOKENS, D)
    k = key_vectors.reshape(TOKENS, D)
    v = value_vectors.reshape(TOKENS, D)
    later, sooner = pl.pallas_call(
        edge_kernel,
        out_shape=[payload(EDGE)] * 2,
        in_specs=[pl.BlockSpec(memory_space=pltpu.HBM)] * 3,
        out_specs=vmem(2),
        scratch_shapes=[
            pltpu.VMEM((TH, TW), jnp.int32),
            pltpu.SemaphoreType.DMA((4 * PAIRS,)),
            pltpu.SemaphoreType.DMA,
        ],
        compiler_params=pltpu.CompilerParams(vmem_limit_bytes=16 << 20),
        cost_estimate=pl.CostEstimate(flops=1 << 16, bytes_accessed=2 << 20, transcendentals=0),
        name="edge",
    )(*(pltpu.with_memory_space_constraint(x, pltpu.HBM) for x in (k, v, land_mask)))
    k, v, land_mask, later, sooner = lax.optimization_barrier((k, v, land_mask, later, sooner))
    later = swapped(later, "lat", 1, True, False)
    sooner = swapped(sooner, "lat", 1, False, False)
    fars = call(far_kernel, "far", [payload(ROWS)] * 4, 1, 3, 1 << 20, 2)(
        offsets, k, v, land_mask
    )
    fars, arrived = list(fars), [None] * 4
    for s in (0, 3, 1, 2):
        if s == 2:
            arrived[3], fars[2] = lax.optimization_barrier((arrived[3], fars[2]))
        arrived[s] = swapped(fars[s], "lon", 2 ** (s // 2 + 1), s % 2 == 1)
    to_cross, to_near = call(
        side_kernel, "side", [payload(2 * SIDE)] * 2, 0, 5, 1 << 33, 3
    )(k, v, land_mask, later, sooner)
    crossed = swapped(to_cross, "lon", 1, True)
    nearby = swapped(to_near, "lon", 1, False)
    line = jax.ShapeDtypeStruct((PAIRS, 8, 2 * TOKENS), jnp.float32)
    partial = call(
        first_kernel, "first", [jax.ShapeDtypeStruct((D, TOKENS), jnp.float32), line, line],
        2, 10, 1 << 34, 6,
        [
            pltpu.VMEM((HALO, 2 * TOKENS, LANES), jnp.float32),
            pltpu.VMEM((4, TOKENS, LANES), jnp.float32),
        ],
        24,
    )(offsets, radius, q, k, v, land_mask, later, sooner, *arrived)
    result = pl.pallas_call(
        second_kernel,
        out_shape=jax.ShapeDtypeStruct((TOKENS, D), jnp.float32),
        in_specs=smem(1) + vmem(6),
        out_specs=pl.BlockSpec(memory_space=pltpu.HBM),
        scratch_shapes=[
            pltpu.VMEM((HALO, TOKENS, LANES), jnp.float32),
            pltpu.VMEM((TOKENS, D), jnp.float32),
            pltpu.SemaphoreType.DMA((PAIRS,)),
        ],
        compiler_params=pltpu.CompilerParams(vmem_limit_bytes=16 << 20),
        cost_estimate=pl.CostEstimate(flops=1 << 28, bytes_accessed=4 << 20, transcendentals=0),
        name="second",
    )(radius, q, crossed, nearby, *partial)
    return result.reshape(TH, TW, D)


def solution(mesh):
    tile = P("lat", "lon", None)
    in_specs = (tile, tile, tile, P("lat", "lon"), P(), P())
    return jax.shard_map(local, mesh=mesh, in_specs=in_specs, out_specs=tile, check_vma=False)
```
